32 devices in a mesh: dp: 8 (over y, x, core), shard: 4 (over z).
Axes of the slice: x: 2, y: 2, z: 4, core: 2. Of those that a mesh axis runs over, the one named last changes fastest.
Arguments:
- momentum: float32 [4096, 7168], P('dp', 'shard'), may hold values from -6 to 6
- gradient: bfloat16 [4096, 7168], P('dp', 'shard'), may hold values from -120 to 120
Outputs:
- new_momentum: float32 [4096, 7168], P('dp', 'shard')
- update: float32 [4096, 7168], P('dp', 'shard')
The draws below stay inside these ranges and needn't reach their ends.
All inputs are finite; a program needn't handle non-finite values.
Results may differ from the reference program's by a relative error of at most 0.0038.
The reference program's roundings to bfloat16 on the way count: a program that leaves them out, or rounds other values in their place, can miss the bound.
Values may be sent and summed in bfloat16 or wider, within the bound.
No kernel may reach another device: no remote copies, remote signals or barrier semaphores. Data moves between devices by JAX's collectives and lax.ppermute only.
A program may use at most 64 MiB of HBM per device.

```python
import math
import jax
import jax.numpy as jnp
from jax import lax

D = 7168
STEPS = 2
ROWS = 4096


def draw_gradient(key, part):
    first_key, second_key, third_key = jax.random.split(jax.random.fold_in(key, 7), 3)
    trend = jnp.exp(jnp.arange(ROWS, dtype=jnp.float32) / ROWS * math.log(3.0))
    row_scale = trend * jnp.exp(jax.random.uniform(second_key, (ROWS,), jnp.float32, 0.0, math.log(10.0)))
    column_scale = jnp.exp(jax.random.uniform(third_key, (D,), jnp.float32, 0.0, math.log(10.0)))
    noise = jnp.clip(jax.random.normal(first_key, (ROWS, D), jnp.float32), -4.0, 4.0)
    values = noise * row_scale[:, None] * column_scale[None, :] / 10.0
    return values.astype(jnp.bfloat16)


def level_of(rng, extent, shards, smallest, largest):
    factor_of, own = 1.0, jax.random.fold_in(rng, 6)
    for position, shards_of in shards:
        steps = jnp.exp(jax.random.uniform(jax.random.fold_in(own, position), (shards_of,), jnp.float32, smallest / len(shards), largest / len(shards)))
        factor_of = factor_of * jnp.repeat(steps, extent[position] // shards_of).reshape([-1 if axis == position else 1 for axis in range(len(extent))])
    return factor_of


def normal_values(key, dims, scale, limit, cuts=(), held_as=jnp.bfloat16):
    loudness = level_of(key, dims, cuts, -0.22, 0.18) if cuts else 1.0
    drawn = jax.random.normal(key, dims, jnp.float32) * scale * loudness
    return jnp.minimum(jnp.maximum(drawn, -limit), limit).astype(held_as)


def setup_inputs(seed: int = 0) -> dict:
    key_list = jax.random.split(jax.random.key(seed), 3)
    momentum = normal_values(key_list[0], (ROWS, D), 1.0, 6.0, ((0, 8), (1, 4)), jnp.float32)
    gradient = draw_gradient(jax.random.fold_in(key_list[2], 71), 0)
    return dict(momentum=momentum, gradient=gradient)


momentum_decay = 0.95
linear_term = 3.4445
cubic_term = -4.775
quintic_term = 2.0315

def reference(momentum, gradient):
    grad_full = gradient.astype(jnp.float32)
    new_momentum = momentum_decay * momentum + grad_full
    current = grad_full + momentum_decay * new_momentum
    for iteration in range(STEPS):
        matrix = current.astype(jnp.bfloat16)
        gram_matrix = jnp.dot(matrix, matrix.T, preferred_element_type=jnp.float32).astype(jnp.bfloat16)
        square_sum = jnp.sum(jnp.square(gram_matrix.astype(jnp.float32)))
        inverse_norm = lax.rsqrt(square_sum)
        root_scale = jnp.sqrt(inverse_norm)
        first_product = jnp.dot(gram_matrix, matrix, preferred_element_type=jnp.float32)
        mixture = (cubic_term * root_scale * matrix.astype(jnp.float32) + quintic_term * root_scale * inverse_norm * first_product).astype(jnp.bfloat16)
        second_product = jnp.dot(gram_matrix, mixture, preferred_element_type=jnp.float32)
        current = linear_term * root_scale * matrix.astype(jnp.float32) + inverse_norm * second_product
    update = math.sqrt(D) * current
    return (new_momentum, update)
```

```python
import functools
import math

import jax
import jax.numpy as jnp
from jax import lax
from jax.sharding import PartitionSpec as P

STEPS = 2


momentum_decay = 0.95
linear_term = 3.4445
cubic_term = -4.775
quintic_term = 2.0315

f32, bf16 = jnp.float32, jnp.bfloat16


def dot_nn(a, b):
    return lax.dot_general(a, b, (((1,), (0,)), ((), ())), preferred_element_type=f32)


def dot_nt(a, b):
    return lax.dot_general(a, b, (((1,), (1,)), ((), ())), preferred_element_type=f32)


def dot_tn(a, b):
    return lax.dot_general(a, b, (((0,), (0,)), ((), ())), preferred_element_type=f32)


def iterate_general(current):
    matrix = current.astype(bf16)
    column_panel = lax.all_gather(matrix, "dp", axis=0, tiled=True)
    summed_part = lax.psum_scatter(dot_nt(matrix, column_panel), "shard", scatter_dimension=0, tiled=True)
    gram_part = summed_part.astype(bf16)
    gram_panel = lax.all_gather(gram_part, "shard", axis=0, tiled=True)
    square_sum = lax.psum(jnp.sum(jnp.square(gram_part.astype(f32))), ("dp", "shard"))
    inverse_norm = lax.rsqrt(square_sum)
    root_scale = jnp.sqrt(inverse_norm)
    matrix_full = matrix.astype(f32)
    first = dot_nn(gram_panel, column_panel)
    mixture = (
        cubic_term * root_scale * matrix_full + quintic_term * root_scale * inverse_norm * first
    ).astype(bf16)
    second = dot_nn(gram_panel, lax.all_gather(mixture, "dp", axis=0, tiled=True))
    return linear_term * root_scale * matrix_full + inverse_norm * second


def x_bit(i):
    return (i >> 1) & 1


def y_bit(i):
    return (i >> 2) & 1


def x_pick(i):
    return i ^ 2 ^ x_bit(i)


def y_pick(i):
    return i ^ 4 ^ (x_bit(i) ^ y_bit(i))


ROW_DEVICES = 8
CORE = [(i, i ^ 1) for i in range(ROW_DEVICES)]
TAKE_X = [(x_pick(i), i) for i in range(ROW_DEVICES)]
TAKE_Y = [(y_pick(i), i) for i in range(ROW_DEVICES)]
GIVE_X = [(i, x_pick(i)) for i in range(ROW_DEVICES)]
GIVE_Y = [(i, y_pick(i)) for i in range(ROW_DEVICES)]


def over_dp(value, pairs):
    return lax.ppermute(value, "dp", pairs)


def gather(block):
    half = block.shape[0] // 2
    core = over_dp(block, CORE)
    x_sel = over_dp(block, TAKE_X)
    y_sel = over_dp(block, TAKE_Y)
    return core, x_sel, y_sel, half


def gather_rest(x_sel, y_sel, half):
    x_oth = over_dp(x_sel, CORE)
    y_oth = over_dp(y_sel, CORE)
    d_sel_top = over_dp(y_sel[:half], GIVE_X)
    d_oth_bottom = over_dp(x_sel[half:], GIVE_Y)
    d_oth_top = over_dp(d_sel_top, CORE)
    d_sel_bottom = over_dp(d_oth_bottom, CORE)
    return x_oth, y_oth, (d_sel_top, d_sel_bottom), (d_oth_top, d_oth_bottom)


def shifted(value, by, size):
    return lax.ppermute(value, "shard", [(z, (z + by) % size) for z in range(size)])


def reduce_part(partial, z, size):
    rows = partial.shape[0] // size
    sent = partial.astype(bf16)
    total = lax.dynamic_slice_in_dim(partial, z * rows, rows, 0)
    for by in range(1, size):
        piece = lax.dynamic_slice_in_dim(sent, (z + by) % size * rows, rows, 0)
        total = total + shifted(piece, by, size).astype(f32)
    return total.astype(bf16)


def spread(part, size):
    return [part] + [shifted(part, by, size) for by in range(1, size)]


def assemble(parts, z, size):
    rows = parts[0].shape[0]
    whole = jnp.zeros((rows * size,) + parts[0].shape[1:], parts[0].dtype)
    for by, part in enumerate(parts):
        whole = lax.dynamic_update_slice_in_dim(whole, part, (z - by) % size * rows, 0)
    return whole


def total_of(value, size):
    value = jnp.broadcast_to(value, (8, 128))
    step = 1
    while step < size:
        value = value + lax.ppermute(value, "shard", [(z, z ^ step) for z in range(size)])
        step *= 2
    for step in (1, 2, 4):
        value = value + over_dp(value, [(i, i ^ step) for i in range(ROW_DEVICES)])
    return value[0, 0]


def square_of(part):
    return jnp.sum(jnp.square(part.astype(f32)))


def product(gram, block, near, rest):
    own_pair, x_nat, y_nat, d_nat, x_tr, y_tr, d_tr = gram
    core, x_sel, y_sel, half = near
    x_oth, y_oth, d_sel, d_oth = rest
    rows = block.shape[0]
    out = dot_nn(own_pair[:, :rows], block) + dot_nn(own_pair[:, rows:], core)
    out = out + dot_nn(x_nat, x_sel) + dot_nn(y_nat, y_sel)
    out = out + dot_tn(x_tr, x_oth) + dot_tn(y_tr, y_oth)
    out = out + dot_nn(d_nat[:, :half], d_sel[0]) + dot_tn(d_tr[:half], d_oth[0])
    out = out + dot_nn(d_nat[:, half:], d_sel[1]) + dot_tn(d_tr[half:], d_oth[1])
    return out


def iterate_square(current, size):
    z = lax.axis_index("shard")
    matrix = current.astype(bf16)
    rows = matrix.shape[0]
    near = gather(matrix)
    core, x_sel, y_sel, half = near
    own = jnp.concatenate([dot_nt(matrix, matrix), dot_nt(matrix, core)], axis=1)
    own_part = reduce_part(own, z, size)
    own_pair = assemble(spread(own_part, size), z, size)
    far = jnp.concatenate([dot_nt(matrix, x_sel), dot_nt(matrix, y_sel), dot_nt(x_sel, y_sel)], axis=1)
    far_part = reduce_part(far, z, size)
    square_sum = total_of(square_of(own_part) + 2.0 * square_of(far_part), size)
    rest = gather_rest(x_sel, y_sel, half)
    parts = spread(far_part, size)
    x_parts = [over_dp(jnp.concatenate([p[:, :rows], p[:, 2 * rows :]], axis=1), GIVE_X) for p in parts]
    y_parts = [over_dp(p[:, rows:], GIVE_Y) for p in parts]
    far_pair = assemble([p[:, : 2 * rows] for p in parts], z, size)
    x_pair = assemble(x_parts, z, size)
    y_pair = assemble(y_parts, z, size)
    gram = (
        own_pair,
        far_pair[:, :rows],
        far_pair[:, rows:],
        x_pair[:, rows:],
        x_pair[:, :rows],
        y_pair[:, :rows],
        y_pair[:, rows:],
    )
    inverse_norm = lax.rsqrt(square_sum)
    root_scale = jnp.sqrt(inverse_norm)
    matrix_full = matrix.astype(f32)
    first = product(gram, matrix, near, rest)
    mixture = (
        cubic_term * root_scale * matrix_full + quintic_term * root_scale * inverse_norm * first
    ).astype(bf16)
    mixture_near = gather(mixture)
    mixture_rest = gather_rest(*mixture_near[1:])
    second = product(gram, mixture, mixture_near, mixture_rest)
    return linear_term * root_scale * matrix_full + inverse_norm * second


def body(iterate, columns, momentum, gradient):
    grad_full = gradient.astype(f32)
    new_momentum = momentum_decay * momentum + grad_full
    current = grad_full + momentum_decay * new_momentum
    for iteration in range(STEPS):
        current = iterate(current)
    return (new_momentum, math.sqrt(columns) * current)


def solution(mesh):
    row_devices, column_devices = mesh.shape["dp"], mesh.shape["shard"]
    spec = P("dp", "shard")

    def step(momentum, gradient):
        rows, columns = momentum.shape
        square = row_devices == ROW_DEVICES and column_devices & (column_devices - 1) == 0
        square = square and rows // row_devices % (column_devices * 32) == 0
        iterate = functools.partial(iterate_square, size=column_devices) if square else iterate_general
        return jax.shard_map(
            functools.partial(body, iterate, columns),
            mesh=mesh,
            in_specs=(spec, spec),
            out_specs=(spec, spec),
            check_vma=False,
        )(momentum, gradient)

    return step
```

```python
import functools
import math

import jax
import jax.numpy as jnp
from jax import lax
from jax.experimental import pallas as pl
from jax.experimental.pallas import tpu as pltpu
from jax.sharding import PartitionSpec as P


STEPS = 2


momentum_decay = 0.95
linear_term = 3.4445
cubic_term = -4.775
quintic_term = 2.0315

f32, bf16 = jnp.float32, jnp.bfloat16


def dot_nn(a, b):
    return lax.dot_general(a, b, (((1,), (0,)), ((), ())), preferred_element_type=f32)


def dot_nt(a, b):
    return lax.dot_general(a, b, (((1,), (1,)), ((), ())), preferred_element_type=f32)


def iterate_general(current):
    matrix = current.astype(bf16)
    column_panel = lax.all_gather(matrix, "dp", axis=0, tiled=True)
    summed_part = lax.psum_scatter(dot_nt(matrix, column_panel), "shard", scatter_dimension=0, tiled=True)
    gram_part = summed_part.astype(bf16)
    gram_panel = lax.all_gather(gram_part, "shard", axis=0, tiled=True)
    square_sum = lax.psum(jnp.sum(jnp.square(gram_part.astype(f32))), ("dp", "shard"))
    inverse_norm = lax.rsqrt(square_sum)
    root_scale = jnp.sqrt(inverse_norm)
    matrix_full = matrix.astype(f32)
    first = dot_nn(gram_panel, column_panel)
    mixture = (
        cubic_term * root_scale * matrix_full + quintic_term * root_scale * inverse_norm * first
    ).astype(bf16)
    second = dot_nn(gram_panel, lax.all_gather(mixture, "dp", axis=0, tiled=True))
    return linear_term * root_scale * matrix_full + inverse_norm * second


def x_bit(i):
    return (i >> 1) & 1


def y_bit(i):
    return (i >> 2) & 1


def x_pick(i):
    return i ^ 2 ^ x_bit(i)


def y_pick(i):
    return i ^ 4 ^ (x_bit(i) ^ y_bit(i))


ROW_DEVICES = 8
VMEM_LIMIT = 20 << 20
CORE = [(i, i ^ 1) for i in range(ROW_DEVICES)]
TAKE_X = [(x_pick(i), i) for i in range(ROW_DEVICES)]
TAKE_Y = [(y_pick(i), i) for i in range(ROW_DEVICES)]
GIVE_X = [(i, x_pick(i)) for i in range(ROW_DEVICES)]
GIVE_Y = [(i, y_pick(i)) for i in range(ROW_DEVICES)]


def over_dp(value, pairs):
    return lax.ppermute(value, "dp", pairs)


def call(kernel, outs, args, specs, out_specs, grid, scratch=(), flops=0, prefetch=0):
    moved = sum(a.size * a.dtype.itemsize for a in args) + sum(o.size * o.dtype.itemsize for o in outs)
    return pl.pallas_call(
        kernel,
        out_shape=outs,
        grid_spec=pltpu.PrefetchScalarGridSpec(
            num_scalar_prefetch=prefetch,
            grid=grid,
            in_specs=specs,
            out_specs=out_specs,
            scratch_shapes=list(scratch),
        ),
        compiler_params=pltpu.CompilerParams(vmem_limit_bytes=VMEM_LIMIT),
        cost_estimate=pl.CostEstimate(flops=flops, bytes_accessed=moved, transcendentals=0),
    )(*args)


def whole_spec(a):
    return pl.BlockSpec(a.shape, lambda *_: (0,) * len(a.shape), pipeline_mode=pl.Buffered(1))


def gram_kernel(pairs, count, size, z_ref, *refs):
    halves, (kept, *pieces), total = refs[:count], refs[count:-1], refs[-1]
    z = z_ref[0]
    rows = kept.shape[1]
    for p, (left, right) in enumerate(pairs):
        value = jnp.concatenate([halves[2 * left][...], halves[2 * left + 1][...]], axis=0)
        half = value.shape[0] // 2
        for h in range(2):
            total[p, :, h * half : (h + 1) * half] = dot_nt(value, halves[2 * right + h][...])
    for by in range(size):
        at = pl.multiple_of(lax.rem(z + by, size) * rows, rows)
        piece = total[:, pl.ds(at, rows), :]
        if by:
            pieces[by - 1][...] = piece.astype(bf16)
        else:
            kept[...] = piece


def gram(z, size, blocks, pairs):
    halves = [half for block in blocks for half in block]
    rows, columns = 2 * halves[0].shape[0], halves[0].shape[1]
    shape = (len(pairs), rows // size, rows)
    outs = [jax.ShapeDtypeStruct(shape, f32)] + [jax.ShapeDtypeStruct(shape, bf16)] * (size - 1)
    return call(
        functools.partial(gram_kernel, pairs, len(halves), size),
        outs,
        [z] + halves,
        [whole_spec(h) for h in halves],
        [pl.BlockSpec(shape, lambda *_: (0, 0, 0), pipeline_mode=pl.Buffered(1))] * size,
        (1,),
        [pltpu.VMEM((len(pairs), rows, rows), f32)],
        2 * len(pairs) * rows * rows * columns,
        1,
    )


def assemble_kernel(takes, size, z_ref, *refs):
    groups, outs = refs[: len(refs) - len(takes)], refs[len(refs) - len(takes) :]
    z = z_ref[0]
    rows = groups[0].shape[1]
    columns = groups[0].shape[2]
    for out, taken in zip(outs, takes):
        for k, (group, index, transposed) in enumerate(taken):
            for by in range(size):
                part = groups[group * size + by][index]
                at = pl.multiple_of(lax.rem(z + size - by, size) * rows, rows)
                if transposed:
                    out[:, pl.ds(pl.multiple_of(k * columns + at, rows), rows)] = part.T
                else:
                    out[pl.ds(at, rows), k * columns : (k + 1) * columns] = part


def assemble(z, size, groups, takes):
    parts = [part for group in groups for part in group]
    columns = parts[0].shape[2]
    outs = [jax.ShapeDtypeStruct((columns, columns * len(taken)), bf16) for taken in takes]
    return call(
        functools.partial(assemble_kernel, takes, size),
        outs,
        [z] + parts,
        [whole_spec(p) for p in parts],
        [pl.BlockSpec(o.shape, lambda *_: (0, 0), pipeline_mode=pl.Buffered(1)) for o in outs],
        (1,),
        prefetch=1,
    )


def product_kernel(n_grams, n_halves, has_sum, finish, *refs):
    refs = list(refs)
    scale_ref = refs.pop(0) if finish else None
    grams, refs = refs[:n_grams], refs[n_grams:]
    halves, refs = refs[:n_halves], refs[n_halves:]
    gram = jnp.concatenate([g[...] for g in grams], axis=1)
    value = dot_nn(gram, jnp.concatenate([h[...] for h in halves], axis=0))
    if has_sum:
        value = value + refs.pop(0)[...]
    if finish:
        own = jnp.concatenate([refs[0][...], refs[1][...]], axis=0)
        value = scale_ref[0] * own.astype(f32) + scale_ref[1] * value
        refs = refs[2:]
    rows = value.shape[0] // len(refs)
    for k, out in enumerate(refs):
        out[...] = value[k * rows : (k + 1) * rows].astype(out.dtype)


def product(grams, blocks, summed=None, finish=None, dtype=f32, parts=1):
    halves = [half for block in blocks for half in block]
    half, columns = halves[0].shape
    tile = 256 if columns % 256 == 0 else columns
    half_spec = pl.BlockSpec((half, tile), lambda t, *_: (0, t))
    row_spec = pl.BlockSpec((2 * half, tile), lambda t, *_: (0, t))
    args = ([finish[0]] if finish else []) + list(grams) + halves
    specs = [whole_spec(g) for g in grams] + [half_spec] * len(halves)
    if summed is not None:
        args, specs = args + [summed], specs + [row_spec]
    if finish:
        args, specs = args + list(finish[1]), specs + [half_spec] * 2
    return call(
        functools.partial(product_kernel, len(grams), len(halves), summed is not None, finish is not None),
        [jax.ShapeDtypeStruct((2 * half // parts, columns), dtype)] * parts,
        args,
        specs,
        [half_spec if parts == 2 else row_spec] * parts,
        (columns // tile,),
        flops=4 * half * half * columns * len(halves),
        prefetch=1 if finish else 0,
    )


def shifted(value, by, size):
    return lax.ppermute(value, "shard", [(z, (z + by) % size) for z in range(size)])


def total_of(value, size):
    value = jnp.broadcast_to(value, (8, 128))
    value = sum([shifted(value, by, size) for by in range(1, size)], value)
    for step in (1, 2, 4):
        value = value + over_dp(value, [(i, i ^ step) for i in range(ROW_DEVICES)])
    return value[0, 0]


def square_of(part):
    return jnp.sum(jnp.square(part.astype(f32)))


def gather(block):
    top, bottom = block
    x_bottom, y_top = over_dp(bottom, TAKE_X), over_dp(top, TAKE_Y)
    x_top, y_bottom = over_dp(top, TAKE_X), over_dp(bottom, TAKE_Y)
    core = over_dp(top, CORE), over_dp(bottom, CORE)
    d_oth_bottom, d_sel_top = over_dp(x_bottom, GIVE_Y), over_dp(y_top, GIVE_X)
    x_oth = over_dp(x_top, CORE), over_dp(x_bottom, CORE)
    y_oth = over_dp(y_top, CORE), over_dp(y_bottom, CORE)
    d_oth_top, d_sel_bottom = over_dp(d_sel_top, CORE), over_dp(d_oth_bottom, CORE)
    near = core, (x_top, x_bottom), (y_top, y_bottom)
    return near, (x_oth, y_oth, (d_sel_top, d_sel_bottom), (d_oth_top, d_oth_bottom))


def reduce_parts(pieces, size):
    kept, *sent = pieces
    total = kept
    for by, piece in enumerate(sent, 1):
        total = total + shifted(piece, by, size).astype(f32)
    return total.astype(bf16)


def spread(part, size):
    return [part] + [shifted(part, by, size) for by in range(1, size)]


def iterate_square(matrix, size, gain, dtype, parts):
    z = lax.axis_index("shard").reshape(1)
    (core, x_sel, y_sel), (x_oth, y_oth, d_sel, d_oth) = gather(matrix)
    own_pieces = gram(z, size, [matrix, core], [(0, 0), (0, 1)])
    own_part = reduce_parts(own_pieces, size)
    own_parts = spread(own_part, size)
    far_pieces = gram(z, size, [matrix, x_sel, y_sel], [(0, 1), (1, 2), (0, 2)])
    far_part = reduce_parts(far_pieces, size)
    square_sum = total_of(square_of(own_part) + 2.0 * square_of(far_part), size)
    far_parts = spread(far_part, size)
    x_parts = [over_dp(p[:2], GIVE_X) for p in far_parts]
    y_parts = [over_dp(p[1:], GIVE_Y) for p in far_parts]
    (own,) = assemble(z, size, [own_parts], [[(0, 0, False), (0, 1, False)]])
    (far,) = assemble(z, size, [far_parts], [[(0, 0, False), (0, 2, False)]])
    side, diagonal = assemble(
        z,
        size,
        [x_parts, y_parts],
        [[(0, 0, True), (1, 1, True)], [(0, 1, False), (1, 0, True)]],
    )
    inverse_norm = lax.rsqrt(square_sum)
    root_scale = jnp.sqrt(inverse_norm)
    (first,) = product([own], [matrix, core])
    (first,) = product([far], [x_sel, y_sel], first)
    scales = jnp.stack([cubic_term * root_scale, quintic_term * root_scale * inverse_norm])
    mixture = product(
        [side, diagonal], [x_oth, y_oth, d_sel, d_oth], first, (scales, matrix), bf16, 2
    )
    (core, x_sel, y_sel), (x_oth, y_oth, d_sel, d_oth) = gather(mixture)
    (second,) = product([own], [mixture, core])
    (second,) = product([far, side], [x_sel, y_sel, x_oth, y_oth], second)
    scales = gain * jnp.stack([linear_term * root_scale, inverse_norm])
    return product([diagonal], [d_sel, d_oth], second, (scales, matrix), dtype, parts)


def current_of(momentum, gradient):
    grad_full = gradient.astype(f32)
    new_momentum = momentum_decay * momentum + grad_full
    return new_momentum, grad_full + momentum_decay * new_momentum


def body_square(size, columns, momentum, gradient):
    half = momentum.shape[0] // 2
    block = [
        current_of(momentum[rows], gradient[rows])[1].astype(bf16)
        for rows in (slice(0, half), slice(half, None))
    ]
    new_momentum, _ = current_of(*lax.optimization_barrier((momentum, gradient)))
    for iteration in range(STEPS):
        last = iteration == STEPS - 1
        block = iterate_square(
            block, size, math.sqrt(columns) if last else 1.0, f32 if last else bf16, 1 if last else 2
        )
    return (new_momentum, block[0])


def body_general(columns, momentum, gradient):
    grad_full = gradient.astype(f32)
    new_momentum = momentum_decay * momentum + grad_full
    current = grad_full + momentum_decay * new_momentum
    for _ in range(STEPS):
        current = iterate_general(current)
    return (new_momentum, math.sqrt(columns) * current)


def solution(mesh):
    row_devices, column_devices = mesh.shape["dp"], mesh.shape["shard"]
    spec = P("dp", "shard")

    def sharded(body):
        return jax.shard_map(body, mesh=mesh, in_specs=(spec, spec), out_specs=(spec, spec), check_vma=False)

    def general(momentum, gradient):
        return sharded(functools.partial(body_general, momentum.shape[1]))(momentum, gradient)

    def square(momentum, gradient):
        return sharded(functools.partial(body_square, column_devices, momentum.shape[1]))(momentum, gradient)

    if row_devices != ROW_DEVICES or column_devices & (column_devices - 1):
        return general
    return square
```

```python
import functools
import math

import jax
import jax.numpy as jnp
from jax import lax
from jax.experimental import pallas as pl
from jax.experimental.pallas import tpu as pltpu
from jax.sharding import PartitionSpec as P


STEPS = 2


momentum_decay = 0.95
linear_term = 3.4445
cubic_term = -4.775
quintic_term = 2.0315

f32, bf16 = jnp.float32, jnp.bfloat16


def dot_nn(a, b):
    return lax.dot_general(a, b, (((1,), (0,)), ((), ())), preferred_element_type=f32)


def dot_nt(a, b):
    return lax.dot_general(a, b, (((1,), (1,)), ((), ())), preferred_element_type=f32)


def iterate_general(current):
    matrix = current.astype(bf16)
    column_panel = lax.all_gather(matrix, "dp", axis=0, tiled=True)
    summed_part = lax.psum_scatter(dot_nt(matrix, column_panel), "shard", scatter_dimension=0, tiled=True)
    gram_part = summed_part.astype(bf16)
    gram_panel = lax.all_gather(gram_part, "shard", axis=0, tiled=True)
    square_sum = lax.psum(jnp.sum(jnp.square(gram_part.astype(f32))), ("dp", "shard"))
    inverse_norm = lax.rsqrt(square_sum)
    root_scale = jnp.sqrt(inverse_norm)
    matrix_full = matrix.astype(f32)
    first = dot_nn(gram_panel, column_panel)
    mixture = (
        cubic_term * root_scale * matrix_full + quintic_term * root_scale * inverse_norm * first
    ).astype(bf16)
    second = dot_nn(gram_panel, lax.all_gather(mixture, "dp", axis=0, tiled=True))
    return linear_term * root_scale * matrix_full + inverse_norm * second


def x_bit(i):
    return (i >> 1) & 1


def y_bit(i):
    return (i >> 2) & 1


def x_pick(i):
    return i ^ 2 ^ x_bit(i)


def y_pick(i):
    return i ^ 4 ^ (x_bit(i) ^ y_bit(i))


ROW_DEVICES = 8
VMEM_LIMIT = 16 << 20
CORE = [(i, i ^ 1) for i in range(ROW_DEVICES)]
TAKE_X = [(x_pick(i), i) for i in range(ROW_DEVICES)]
TAKE_Y = [(y_pick(i), i) for i in range(ROW_DEVICES)]
GIVE_X = [(i, x_pick(i)) for i in range(ROW_DEVICES)]
GIVE_Y = [(i, y_pick(i)) for i in range(ROW_DEVICES)]


def over_dp(value, pairs):
    return lax.ppermute(value, "dp", pairs)


def call(kernel, outs, args, scalars=(), scratch=(), flops=0):
    moved = sum(a.size * a.dtype.itemsize for a in [*args, *outs])
    vmem = pl.BlockSpec(memory_space=pltpu.VMEM)
    return pl.pallas_call(
        kernel,
        out_shape=outs,
        in_specs=[pl.BlockSpec(memory_space=pltpu.SMEM)] * len(scalars) + [vmem] * len(args),
        out_specs=[vmem] * len(outs),
        scratch_shapes=list(scratch),
        compiler_params=pltpu.CompilerParams(vmem_limit_bytes=VMEM_LIMIT),
        cost_estimate=pl.CostEstimate(flops=flops, bytes_accessed=moved, transcendentals=0),
    )(*scalars, *[pltpu.with_memory_space_constraint(a, pltpu.VMEM) for a in args])


def split_rows(total, size, z, kept, pieces):
    rows = kept.shape[1]
    for by in range(size):
        at = pl.multiple_of(lax.rem(z + by, size) * rows, rows)
        piece = total[:, pl.ds(at, rows), :]
        if by:
            pieces[by - 1][...] = piece.astype(bf16)
        else:
            kept[...] = piece


def own_gram_kernel(size, z_ref, core_ref, top, bottom, core_top, core_bottom, kept, *rest):
    pieces, total = rest[:-1], rest[-1]
    for q, (left, right) in enumerate([(top, top), (bottom, bottom), (bottom, top)]):
        total[q] = dot_nt(left[...], right[...])
    for core, (first, second) in enumerate([(core_top, core_bottom), (core_bottom, core_top)]):

        @pl.when(core_ref[0] == core)
        def _():
            total[3] = dot_nt(top[...], first[...])
            total[4] = dot_nt(bottom[...], second[...])

    split_rows(total, size, z_ref[0], kept, pieces)


def far_gram_kernel(size, z_ref, *refs):
    halves, (kept, *pieces), total = refs[:6], refs[6:-1], refs[-1]
    for p, (left, right) in enumerate([(0, 1), (1, 2), (0, 2)]):
        value = jnp.concatenate([halves[2 * left][...], halves[2 * left + 1][...]], axis=0)
        half = value.shape[0] // 2
        for h in range(2):
            total[p, :, h * half : (h + 1) * half] = dot_nt(value, halves[2 * right + h][...])
    split_rows(total, size, z_ref[0], kept, pieces)


def gram(kernel, shape, size, scalars, blocks):
    halves = [half for block in blocks for half in block]
    count, rows, columns = shape
    shape = (count, rows // size, columns)
    outs = [jax.ShapeDtypeStruct(shape, f32)] + [jax.ShapeDtypeStruct(shape, bf16)] * (size - 1)
    return call(
        functools.partial(kernel, size),
        outs,
        halves,
        scalars,
        [pltpu.VMEM((count, rows, columns), f32)],
        2 * count * rows * columns * halves[0].shape[1],
    )


def own_assemble_kernel(size, z_ref, *refs):
    parts, (diagonal, beside) = refs[:-2], refs[-2:]
    z = z_ref[0]
    rows, half = parts[0].shape[1], parts[0].shape[2]
    for by, part in enumerate(parts):
        at = lax.rem(z + size - by, size) * rows
        upper, lower = pl.ds(pl.multiple_of(at, rows), rows), pl.ds(pl.multiple_of(half + at, rows), rows)
        diagonal[upper, :half] = part[0]
        diagonal[lower, half:] = part[1]
        diagonal[lower, :half] = part[2]
        beside[upper, :] = part[3]
        beside[lower, :] = part[4]
    diagonal[:half, half:] = diagonal[half:, :half].T


def own_assemble(z, size, parts):
    half = parts[0].shape[2]
    outs = [jax.ShapeDtypeStruct((2 * half, columns), bf16) for columns in (2 * half, half)]
    return call(functools.partial(own_assemble_kernel, size), outs, parts, [z])


def beside_kernel(core_ref, own, other, out):
    half = own.shape[1]
    for core in range(2):

        @pl.when(core_ref[0] == core)
        def _():
            like, unlike = slice(core * half, (core + 1) * half), slice((1 - core) * half, (2 - core) * half)
            out[:half, like] = own[:half]
            out[half:, unlike] = own[half:]
            out[unlike, :half] = other[:half].T
            out[like, half:] = other[half:].T


def beside_of(core, own, other):
    rows = own.shape[0]
    return call(beside_kernel, [jax.ShapeDtypeStruct((rows, rows), bf16)], [own, other], [core])[0]


def assemble_kernel(takes, size, z_ref, *refs):
    groups, outs = refs[: len(refs) - len(takes)], refs[len(refs) - len(takes) :]
    z = z_ref[0]
    rows = groups[0].shape[1]
    columns = groups[0].shape[2]
    for out, taken in zip(outs, takes):
        for k, (group, index, transposed) in enumerate(taken):
            for by in range(size):
                part = groups[group * size + by][index]
                at = pl.multiple_of(lax.rem(z + size - by, size) * rows, rows)
                if transposed:
                    out[:, pl.ds(pl.multiple_of(k * columns + at, rows), rows)] = part.T
                else:
                    out[pl.ds(at, rows), k * columns : (k + 1) * columns] = part


def assemble(z, size, groups, takes):
    parts = [part for group in groups for part in group]
    columns = parts[0].shape[2]
    outs = [jax.ShapeDtypeStruct((columns, columns * len(taken)), bf16) for taken in takes]
    return call(functools.partial(assemble_kernel, takes, size), outs, parts, [z])


def product_kernel(n_grams, n_halves, has_sum, finish, tile, *refs):
    refs = list(refs)
    if finish:
        inverse_norm = lax.rsqrt(jnp.sum(refs.pop(0)[...], axis=(0, 1), keepdims=True))
        root_scale = jnp.sqrt(inverse_norm)
        scales = finish(root_scale, inverse_norm)
    grams, refs = refs[:n_grams], refs[n_grams:]
    halves, refs = refs[:n_halves], refs[n_halves:]
    summed = refs.pop(0) if has_sum else None
    own, outs = (refs[:2], refs[2:]) if finish else (None, refs)
    columns = halves[0].shape[1]

    def column_tile(t, carry):
        at = pl.ds(pl.multiple_of(t * tile, tile), tile)
        gram = jnp.concatenate([g[...] for g in grams], axis=1)
        value = dot_nn(gram, jnp.concatenate([h[:, at] for h in halves], axis=0))
        if has_sum:
            value = value + summed[:, at]
        if finish:
            block = jnp.concatenate([own[0][:, at], own[1][:, at]], axis=0)
            value = scales[0] * block.astype(f32) + scales[1] * value
        rows = value.shape[0] // len(outs)
        for k, out in enumerate(outs):
            out[:, at] = value[k * rows : (k + 1) * rows].astype(out.dtype)
        return carry

    lax.fori_loop(0, columns // tile, column_tile, 0)


def product(grams, blocks, summed=None, finish=None, dtype=f32, parts=1):
    halves = [half for block in blocks for half in block]
    half, columns = halves[0].shape
    tile = 256 if columns % 256 == 0 else columns
    args = ([finish[1]] if finish else []) + list(grams) + halves
    args += [] if summed is None else [summed]
    args += list(finish[2]) if finish else []
    outs = [jax.ShapeDtypeStruct((2 * half // parts, columns), dtype)] * parts
    return call(
        functools.partial(
            product_kernel, len(grams), len(halves), summed is not None, finish and finish[0], tile
        ),
        outs,
        args,
        flops=4 * half * half * columns * len(halves),
    )


def shifted(value, by, size):
    return lax.ppermute(value, "shard", [(z, (z + by) % size) for z in range(size)])


def total_of(value, size):
    for step in (1, 2, 4):
        value = value + over_dp(value, [(i, i ^ step) for i in range(ROW_DEVICES)])
    return sum([shifted(value, by, size) for by in range(1, size)], value)


def gather(block):
    top, bottom = block
    x_bottom, y_top = over_dp(bottom, TAKE_X), over_dp(top, TAKE_Y)
    x_top, y_bottom = over_dp(top, TAKE_X), over_dp(bottom, TAKE_Y)
    core = over_dp(top, CORE), over_dp(bottom, CORE)
    d_oth_bottom, d_sel_top = over_dp(x_bottom, GIVE_Y), over_dp(y_top, GIVE_X)
    x_oth = over_dp(x_top, CORE), over_dp(x_bottom, CORE)
    y_oth = over_dp(y_top, CORE), over_dp(y_bottom, CORE)
    d_oth_top, d_sel_bottom = over_dp(d_sel_top, CORE), over_dp(d_oth_bottom, CORE)
    near = core, (x_top, x_bottom), (y_top, y_bottom)
    return near, (x_oth, y_oth, (d_sel_top, d_sel_bottom), (d_oth_top, d_oth_bottom))


def fold_kernel(weights, *refs):
    kept, *pieces, before, out, squares = refs
    total = kept[...]
    for piece in pieces:
        total = total + piece[...].astype(f32)
    part = total.astype(bf16)
    out[...] = part
    total = before[...]
    for index, weight in enumerate(weights):
        square = jnp.square(part[index].astype(f32))
        square = sum(square[:, k : k + 128] for k in range(0, square.shape[1], 128))
        total = total + weight * jnp.sum(square.reshape(-1, 8, 128), axis=0)
    squares[...] = total


def reduce_parts(pieces, size, before, weights):
    kept, *sent = pieces
    received = [shifted(piece, by, size) for by, piece in enumerate(sent, 1)]
    outs = [jax.ShapeDtypeStruct(kept.shape, bf16), jax.ShapeDtypeStruct(before.shape, f32)]
    return call(functools.partial(fold_kernel, weights), outs, [kept, *received, before])


def spread(part, size):
    parts = [part]
    for by in range(1, size):
        parts.append(shifted(part, by, size))
    return parts


def iterate_square(matrix, size, gain, dtype, parts):
    z = lax.axis_index("shard").reshape(1)
    side_index = (lax.axis_index("dp") & 1).reshape(1)
    (core, x_sel, y_sel), (x_oth, y_oth, d_sel, d_oth) = gather(matrix)
    half = matrix[0].shape[0]
    own_pieces = gram(own_gram_kernel, (5, half, half), size, [z, side_index], [matrix, core])
    own_part, squares = reduce_parts(
        own_pieces, size, jnp.zeros((8, 128), f32), (1.0, 1.0, 2.0, 2.0, 2.0)
    )
    own_parts = spread(own_part, size)
    far_pieces = gram(far_gram_kernel, (3, 2 * half, 2 * half), size, [z], [matrix, x_sel, y_sel])
    far_part, squares = reduce_parts(far_pieces, size, squares, (2.0, 2.0, 2.0))
    squares = total_of(squares, size)
    far_parts = spread(far_part, size)
    x_parts = [over_dp(p[:2], GIVE_X) for p in far_parts]
    y_parts = [over_dp(p[1:], GIVE_Y) for p in far_parts]
    own, beside = own_assemble(z, size, own_parts)
    beside = beside_of(side_index, beside, over_dp(beside, CORE))
    (far,) = assemble(z, size, [far_parts], [[(0, 0, False), (0, 2, False)]])
    side, diagonal = assemble(
        z,
        size,
        [x_parts, y_parts],
        [[(0, 0, True), (1, 1, True)], [(0, 1, False), (1, 0, True)]],
    )
    (first,) = product([own, beside], [matrix, core])
    (first,) = product([far], [x_sel, y_sel], first)

    def mixing(root_scale, inverse_norm):
        return cubic_term * root_scale, quintic_term * root_scale * inverse_norm

    def ending(root_scale, inverse_norm):
        return gain * linear_term * root_scale, gain * inverse_norm

    mixture = product(
        [side, diagonal], [x_oth, y_oth, d_sel, d_oth], first, (mixing, squares, matrix), bf16, 2
    )
    (core, x_sel, y_sel), (x_oth, y_oth, d_sel, d_oth) = gather(mixture)
    (second,) = product([own, beside], [mixture, core])
    (second,) = product([far, side], [x_sel, y_sel, x_oth, y_oth], second)
    return product([diagonal], [d_sel, d_oth], second, (ending, squares, matrix), dtype, parts)


def current_of(momentum, gradient):
    grad_full = gradient.astype(f32)
    new_momentum = momentum_decay * momentum + grad_full
    return new_momentum, grad_full + momentum_decay * new_momentum


def body_square(size, columns, momentum, gradient):
    half = momentum.shape[0] // 2
    block = [
        current_of(momentum[rows], gradient[rows])[1].astype(bf16)
        for rows in (slice(0, half), slice(half, None))
    ]
    new_momentum, _ = current_of(*lax.optimization_barrier((momentum, gradient)))
    for iteration in range(STEPS):
        last = iteration == STEPS - 1
        block = iterate_square(
            block, size, math.sqrt(columns) if last else 1.0, f32 if last else bf16, 1 if last else 2
        )
    return (new_momentum, block[0])


def body_general(columns, momentum, gradient):
    grad_full = gradient.astype(f32)
    new_momentum = momentum_decay * momentum + grad_full
    current = grad_full + momentum_decay * new_momentum
    for _ in range(STEPS):
        current = iterate_general(current)
    return (new_momentum, math.sqrt(columns) * current)


def solution(mesh):
    row_devices, column_devices = mesh.shape["dp"], mesh.shape["shard"]
    spec = P("dp", "shard")

    def sharded(body):
        return jax.shard_map(body, mesh=mesh, in_specs=(spec, spec), out_specs=(spec, spec), check_vma=False)

    def general(momentum, gradient):
        return sharded(functools.partial(body_general, momentum.shape[1]))(momentum, gradient)

    def square(momentum, gradient):
        return sharded(functools.partial(body_square, column_devices, momentum.shape[1]))(momentum, gradient)

    if row_devices != ROW_DEVICES or column_devices & (column_devices - 1):
        return general
    return square
```

```python
import functools
import math

import jax
import jax.numpy as jnp
from jax import lax
from jax.experimental import pallas as pl
from jax.experimental.pallas import tpu as pltpu
from jax.sharding import PartitionSpec as P


STEPS = 2


momentum_decay = 0.95
linear_term = 3.4445
cubic_term = -4.775
quintic_term = 2.0315

f32, bf16 = jnp.float32, jnp.bfloat16


def dot_nn(a, b):
    return lax.dot_general(a, b, (((1,), (0,)), ((), ())), preferred_element_type=f32)


def dot_nt(a, b):
    return lax.dot_general(a, b, (((1,), (1,)), ((), ())), preferred_element_type=f32)


def iterate_general(current):
    matrix = current.astype(bf16)
    column_panel = lax.all_gather(matrix, "dp", axis=0, tiled=True)
    summed_part = lax.psum_scatter(dot_nt(matrix, column_panel), "shard", scatter_dimension=0, tiled=True)
    gram_part = summed_part.astype(bf16)
    gram_panel = lax.all_gather(gram_part, "shard", axis=0, tiled=True)
    square_sum = lax.psum(jnp.sum(jnp.square(gram_part.astype(f32))), ("dp", "shard"))
    inverse_norm = lax.rsqrt(square_sum)
    root_scale = jnp.sqrt(inverse_norm)
    matrix_full = matrix.astype(f32)
    first = dot_nn(gram_panel, column_panel)
    mixture = (
        cubic_term * root_scale * matrix_full + quintic_term * root_scale * inverse_norm * first
    ).astype(bf16)
    second = dot_nn(gram_panel, lax.all_gather(mixture, "dp", axis=0, tiled=True))
    return linear_term * root_scale * matrix_full + inverse_norm * second


def x_bit(i):
    return (i >> 1) & 1


def y_bit(i):
    return (i >> 2) & 1


def x_pick(i):
    return i ^ 2 ^ x_bit(i)


def y_pick(i):
    return i ^ 4 ^ (x_bit(i) ^ y_bit(i))


ROW_DEVICES = 8
VMEM_LIMIT = 16 << 20
CORE = [(i, i ^ 1) for i in range(ROW_DEVICES)]
TAKE_X = [(x_pick(i), i) for i in range(ROW_DEVICES)]
TAKE_Y = [(y_pick(i), i) for i in range(ROW_DEVICES)]
GIVE_X = [(i, x_pick(i)) for i in range(ROW_DEVICES)]
GIVE_Y = [(i, y_pick(i)) for i in range(ROW_DEVICES)]


def over_dp(value, pairs):
    return lax.ppermute(value, "dp", pairs)


def call(kernel, outs, args, scalars=(), scratch=(), flops=0):
    moved = sum(a.size * a.dtype.itemsize for a in [*args, *outs])
    vmem = pl.BlockSpec(memory_space=pltpu.VMEM)
    return pl.pallas_call(
        kernel,
        out_shape=outs,
        in_specs=[pl.BlockSpec(memory_space=pltpu.SMEM)] * len(scalars) + [vmem] * len(args),
        out_specs=[vmem] * len(outs),
        scratch_shapes=list(scratch),
        compiler_params=pltpu.CompilerParams(vmem_limit_bytes=VMEM_LIMIT),
        cost_estimate=pl.CostEstimate(flops=flops, bytes_accessed=moved, transcendentals=0),
    )(*scalars, *[pltpu.with_memory_space_constraint(a, pltpu.VMEM) for a in args])


def split_rows(total, size, z, kept, pieces):
    rows = kept.shape[1]
    for by in range(size):
        at = pl.multiple_of(lax.rem(z + by, size) * rows, rows)
        piece = total[:, pl.ds(at, rows), :]
        if by:
            pieces[by - 1][...] = piece.astype(bf16)
        else:
            kept[...] = piece


def own_gram_kernel(size, z_ref, core_ref, top, bottom, core_top, core_bottom, kept, *rest):
    pieces, total = rest[:-1], rest[-1]
    for q, (left, right) in enumerate([(top, top), (bottom, bottom), (bottom, top)]):
        total[q] = dot_nt(left[...], right[...])
    for core, (first, second) in enumerate([(core_top, core_bottom), (core_bottom, core_top)]):

        @pl.when(core_ref[0] == core)
        def _():
            total[3] = dot_nt(top[...], first[...])
            total[4] = dot_nt(bottom[...], second[...])

    split_rows(total, size, z_ref[0], kept, pieces)


def stacked(top, bottom):
    return jnp.concatenate([top[...], bottom[...]], axis=0)


def early_gram_kernel(size, z_ref, top, bottom, x_bottom, y_top, kept, *rest):
    pieces, total = rest[:-1], rest[-1]
    half = top.shape[0]
    own = stacked(top, bottom)
    for q, right in ((0, x_bottom), (3, y_top)):
        value = dot_nt(own, right[...])
        total[q], total[q + 1] = value[:half], value[half:]
    total[2] = dot_nt(x_bottom[...], y_top[...])
    split_rows(total, size, z_ref[0], kept, pieces)


def late_gram_kernel(size, z_ref, top, bottom, x_top, x_bottom, y_top, y_bottom, kept, *rest):
    pieces, total = rest[:-1], rest[-1]
    half = top.shape[0]
    own = stacked(top, bottom)
    for q, right in ((0, x_top), (5, y_bottom)):
        value = dot_nt(own, right[...])
        total[q], total[q + 1] = value[:half], value[half:]
    total[2] = dot_nt(x_top[...], y_top[...])
    value = dot_nt(stacked(x_top, x_bottom), y_bottom[...])
    total[3], total[4] = value[:half], value[half:]
    split_rows(total, size, z_ref[0], kept, pieces)


def gram(kernel, shape, size, scalars, halves):
    count, rows, columns = shape
    shape = (count, rows // size, columns)
    outs = [jax.ShapeDtypeStruct(shape, f32)] + [jax.ShapeDtypeStruct(shape, bf16)] * (size - 1)
    return call(
        functools.partial(kernel, size),
        outs,
        halves,
        scalars,
        [pltpu.VMEM((count, rows, columns), f32)],
        2 * count * rows * columns * halves[0].shape[1],
    )


def own_assemble_kernel(size, z_ref, *refs):
    parts, (diagonal, beside) = refs[:-2], refs[-2:]
    z = z_ref[0]
    rows, half = parts[0].shape[1], parts[0].shape[2]
    for by, part in enumerate(parts):
        at = lax.rem(z + size - by, size) * rows
        upper, lower = pl.ds(pl.multiple_of(at, rows), rows), pl.ds(pl.multiple_of(half + at, rows), rows)
        diagonal[upper, :half] = part[0]
        diagonal[lower, half:] = part[1]
        diagonal[lower, :half] = part[2]
        beside[upper, :] = part[3]
        beside[lower, :] = part[4]
    diagonal[:half, half:] = diagonal[half:, :half].T


def own_assemble(z, size, parts):
    half = parts[0].shape[2]
    outs = [jax.ShapeDtypeStruct((2 * half, columns), bf16) for columns in (2 * half, half)]
    return call(functools.partial(own_assemble_kernel, size), outs, parts, [z])


def beside_kernel(core_ref, own, other, out):
    half = own.shape[1]
    for core in range(2):

        @pl.when(core_ref[0] == core)
        def _():
            like, unlike = slice(core * half, (core + 1) * half), slice((1 - core) * half, (2 - core) * half)
            out[:half, like] = own[:half]
            out[half:, unlike] = own[half:]
            out[unlike, :half] = other[:half].T
            out[like, half:] = other[half:].T


def beside_of(core, own, other):
    rows = own.shape[0]
    return call(beside_kernel, [jax.ShapeDtypeStruct((rows, rows), bf16)], [own, other], [core])[0]


def rows_at(z, by, size, rows):
    return pl.multiple_of(lax.rem(z + size - by, size) * rows, rows)


def near_assemble_kernel(size, z_ref, *refs):
    parts, near, wholes = refs[:size], refs[size], refs[size + 1 :]
    count, rows, half = parts[0].shape
    for by, part in enumerate(parts):
        at = rows_at(z_ref[0], by, size, rows)
        lower = pl.multiple_of(half + at, rows)
        near[pl.ds(at, rows), :half] = part[0]
        near[pl.ds(lower, rows), :half] = part[1]
        near[pl.ds(at, rows), half:] = part[count - 2]
        near[pl.ds(lower, rows), half:] = part[count - 1]
        for k, whole in enumerate(wholes):
            whole[:, pl.ds(at, rows), :] = part[2 * k : count - 2 + 2 * k]


def near_assemble(z, size, parts, with_wholes):
    count, _, half = parts[0].shape
    outs = [jax.ShapeDtypeStruct((2 * half, 2 * half), bf16)]
    if with_wholes:
        outs += [jax.ShapeDtypeStruct((count - 2, half, half), bf16)] * 2
    return call(functools.partial(near_assemble_kernel, size), outs, parts, [z])


def mirror_assemble_kernel(size, z_ref, *refs):
    (x_early, y_early), refs = refs[:2], refs[2:]
    x_parts, y_parts, refs = refs[:size], refs[size : 2 * size], refs[2 * size :]
    side, linked, crossed, x_late, y_late = refs
    rows, half = x_parts[0].shape[1:]
    for by in range(size):
        at = pl.ds(rows_at(z_ref[0], by, size, rows), rows)
        x_late[:, at, :] = x_parts[by][...]
        y_late[:, at, :] = y_parts[by][...]
    columns = [slice(k * half, (k + 1) * half) for k in range(4)]
    top, bottom = columns[0], columns[1]
    for k in range(2):
        side[top, columns[k]] = x_late[k].T
        side[bottom, columns[k]] = x_early[k].T
        side[top, columns[2 + k]] = y_early[1 + k].T
        side[bottom, columns[2 + k]] = y_late[3 + k].T
    linked[top, top] = x_late[2]
    linked[bottom, top] = x_early[2]
    linked[top, bottom] = y_early[0].T
    linked[bottom, bottom] = y_late[2].T
    crossed[top, top] = x_late[3]
    crossed[bottom, top] = x_late[4]
    crossed[top, bottom] = y_late[0].T
    crossed[bottom, bottom] = y_late[1].T


def mirror_assemble(z, size, early, x_parts, y_parts):
    count, _, half = x_parts[0].shape
    outs = [jax.ShapeDtypeStruct((2 * half, width * half), bf16) for width in (4, 2, 2)]
    return call(
        functools.partial(mirror_assemble_kernel, size),
        outs,
        [*early, *x_parts, *y_parts],
        [z],
        [pltpu.VMEM((count, half, half), bf16)] * 2,
    )


def product_kernel(n_grams, n_halves, has_sum, finish, tile, *refs):
    refs = list(refs)
    if finish:
        inverse_norm = lax.rsqrt(jnp.sum(refs.pop(0)[...], axis=(0, 1), keepdims=True))
        root_scale = jnp.sqrt(inverse_norm)
        scales = finish(root_scale, inverse_norm)
    grams, refs = refs[:n_grams], refs[n_grams:]
    halves, refs = refs[:n_halves], refs[n_halves:]
    summed = refs.pop(0) if has_sum else None
    own, outs = (refs[:2], refs[2:]) if finish else (None, refs)
    columns = halves[0].shape[1]

    def column_tile(t, carry):
        at = pl.ds(pl.multiple_of(t * tile, tile), tile)
        gram = jnp.concatenate([g[...] for g in grams], axis=1)
        value = dot_nn(gram, jnp.concatenate([h[:, at] for h in halves], axis=0))
        if has_sum:
            value = value + summed[:, at]
        if finish:
            block = jnp.concatenate([own[0][:, at], own[1][:, at]], axis=0)
            value = scales[0] * block.astype(f32) + scales[1] * value
        rows = value.shape[0] // len(outs)
        for k, out in enumerate(outs):
            out[:, at] = value[k * rows : (k + 1) * rows].astype(out.dtype)
        return carry

    lax.fori_loop(0, columns // tile, column_tile, 0)


def product(grams, halves, summed=None, finish=None, dtype=f32, parts=1):
    half, columns = halves[0].shape
    tile = 256 if columns % 256 == 0 else columns
    args = ([finish[1]] if finish else []) + list(grams) + list(halves)
    args += [] if summed is None else [summed]
    args += list(finish[2]) if finish else []
    outs = [jax.ShapeDtypeStruct((2 * half // parts, columns), dtype)] * parts
    return call(
        functools.partial(
            product_kernel, len(grams), len(halves), summed is not None, finish and finish[0], tile
        ),
        outs,
        args,
        flops=4 * half * half * columns * len(halves),
    )


def shifted(value, by, size):
    return lax.ppermute(value, "shard", [(z, (z + by) % size) for z in range(size)])


def total_of(value, size):
    for step in (1, 2, 4):
        value = value + over_dp(value, [(i, i ^ step) for i in range(ROW_DEVICES)])
    return sum([shifted(value, by, size) for by in range(1, size)], value)


def gather(block):
    top, bottom = block
    x_bottom, y_top = over_dp(bottom, TAKE_X), over_dp(top, TAKE_Y)
    x_top, y_bottom = over_dp(top, TAKE_X), over_dp(bottom, TAKE_Y)
    core = over_dp(top, CORE), over_dp(bottom, CORE)
    d_oth_bottom, d_sel_top = over_dp(x_bottom, GIVE_Y), over_dp(y_top, GIVE_X)
    side = [over_dp(half, CORE) for half in (x_top, x_bottom, y_top, y_bottom)]
    crossed = over_dp(d_oth_bottom, CORE), over_dp(d_sel_top, CORE)
    return core, (x_bottom, y_top), (x_top, y_bottom), side, (d_sel_top, d_oth_bottom), crossed


def fold_kernel(weights, *refs):
    kept, *pieces, before, out, squares = refs
    total = kept[...]
    for piece in pieces:
        total = total + piece[...].astype(f32)
    part = total.astype(bf16)
    out[...] = part
    total = before[...]
    for index, weight in enumerate(weights):
        square = jnp.square(part[index].astype(f32))
        square = sum(square[:, k : k + 128] for k in range(0, square.shape[1], 128))
        total = total + weight * jnp.sum(square.reshape(-1, 8, 128), axis=0)
    squares[...] = total


def reduce_parts(pieces, size, before, weights):
    kept, *sent = pieces
    received = [shifted(piece, by, size) for by, piece in enumerate(sent, 1)]
    outs = [jax.ShapeDtypeStruct(kept.shape, bf16), jax.ShapeDtypeStruct(before.shape, f32)]
    return call(functools.partial(fold_kernel, weights), outs, [kept, *received, before])


def spread(part, size):
    parts = [part]
    for by in range(1, size):
        parts.append(shifted(part, by, size))
    return parts


def iterate_square(matrix, size, gain, dtype, parts):
    z = lax.axis_index("shard").reshape(1)
    side_index = (lax.axis_index("dp") & 1).reshape(1)
    core, one, two, side, linked, crossed = gather(matrix)
    (x_bottom, y_top), (x_top, y_bottom) = one, two
    half = matrix[0].shape[0]
    own_pieces = gram(own_gram_kernel, (5, half, half), size, [z, side_index], [*matrix, *core])
    own_part, squares = reduce_parts(
        own_pieces, size, jnp.zeros((8, 128), f32), (1.0, 1.0, 2.0, 2.0, 2.0)
    )
    own_parts = spread(own_part, size)
    early_pieces = gram(early_gram_kernel, (5, half, half), size, [z], [*matrix, x_bottom, y_top])
    early_part, squares = reduce_parts(early_pieces, size, squares, (2.0,) * 5)
    late_pieces = gram(
        late_gram_kernel, (7, half, half), size, [z], [*matrix, x_top, x_bottom, y_top, y_bottom]
    )
    late_part, squares = reduce_parts(late_pieces, size, squares, (2.0,) * 7)
    squares = total_of(squares, size)
    early_parts = spread(early_part, size)
    late_parts = spread(late_part, size)
    near_one, x_whole, y_whole = near_assemble(z, size, early_parts, True)
    early = over_dp(x_whole, GIVE_X), over_dp(y_whole, GIVE_Y)
    x_parts = [over_dp(p[:-2], GIVE_X) for p in late_parts]
    y_parts = [over_dp(p[2:], GIVE_Y) for p in late_parts]
    own, beside = own_assemble(z, size, own_parts)
    beside = beside_of(side_index, beside, over_dp(beside, CORE))
    (near_two,) = near_assemble(z, size, late_parts, False)
    side_gram, linked_gram, crossed_gram = mirror_assemble(z, size, early, x_parts, y_parts)

    def mixing(root_scale, inverse_norm):
        return cubic_term * root_scale, quintic_term * root_scale * inverse_norm

    def ending(root_scale, inverse_norm):
        return gain * linear_term * root_scale, gain * inverse_norm

    (first,) = product([own, beside], [*matrix, *core])
    (first,) = product([near_one, near_two], [*one, *two], first)
    mixture = product(
        [side_gram, linked_gram, crossed_gram],
        [*side, *linked, *crossed],
        first,
        (mixing, squares, matrix),
        bf16,
        2,
    )
    core, one, two, side, linked, crossed = gather(mixture)
    (second,) = product([own, beside], [*mixture, *core])
    (second,) = product([near_one, near_two, side_gram], [*one, *two, *side], second)
    (second,) = product([linked_gram], linked, second)
    return product([crossed_gram], crossed, second, (ending, squares, matrix), dtype, parts)


def current_of(momentum, gradient):
    grad_full = gradient.astype(f32)
    new_momentum = momentum_decay * momentum + grad_full
    return new_momentum, grad_full + momentum_decay * new_momentum


def body_square(size, columns, momentum, gradient):
    half = momentum.shape[0] // 2
    block = [
        current_of(momentum[rows], gradient[rows])[1].astype(bf16)
        for rows in (slice(0, half), slice(half, None))
    ]
    new_momentum, _ = current_of(*lax.optimization_barrier((momentum, gradient)))
    for iteration in range(STEPS):
        last = iteration == STEPS - 1
        block = iterate_square(
            block, size, math.sqrt(columns) if last else 1.0, f32 if last else bf16, 1 if last else 2
        )
    return (new_momentum, block[0])


def body_general(columns, momentum, gradient):
    grad_full = gradient.astype(f32)
    new_momentum = momentum_decay * momentum + grad_full
    current = grad_full + momentum_decay * new_momentum
    for _ in range(STEPS):
        current = iterate_general(current)
    return (new_momentum, math.sqrt(columns) * current)


def solution(mesh):
    row_devices, column_devices = mesh.shape["dp"], mesh.shape["shard"]
    spec = P("dp", "shard")

    def sharded(body):
        return jax.shard_map(body, mesh=mesh, in_specs=(spec, spec), out_specs=(spec, spec), check_vma=False)

    def general(momentum, gradient):
        return sharded(functools.partial(body_general, momentum.shape[1]))(momentum, gradient)

    def square(momentum, gradient):
        return sharded(functools.partial(body_square, column_devices, momentum.shape[1]))(momentum, gradient)

    if row_devices != ROW_DEVICES or column_devices & (column_devices - 1):
        return general
    return square
```

```python
import functools
import math

import jax
import jax.numpy as jnp
from jax import lax
from jax.experimental import pallas as pl
from jax.experimental.pallas import tpu as pltpu
from jax.sharding import PartitionSpec as P


STEPS = 2


momentum_decay = 0.95
linear_term = 3.4445
cubic_term = -4.775
quintic_term = 2.0315

f32, bf16 = jnp.float32, jnp.bfloat16


def dot_nn(a, b):
    return lax.dot_general(a, b, (((1,), (0,)), ((), ())), preferred_element_type=f32)


def dot_nt(a, b):
    return lax.dot_general(a, b, (((1,), (1,)), ((), ())), preferred_element_type=f32)


def iterate_general(current):
    matrix = current.astype(bf16)
    column_panel = lax.all_gather(matrix, "dp", axis=0, tiled=True)
    summed_part = lax.psum_scatter(dot_nt(matrix, column_panel), "shard", scatter_dimension=0, tiled=True)
    gram_part = summed_part.astype(bf16)
    gram_panel = lax.all_gather(gram_part, "shard", axis=0, tiled=True)
    square_sum = lax.psum(jnp.sum(jnp.square(gram_part.astype(f32))), ("dp", "shard"))
    inverse_norm = lax.rsqrt(square_sum)
    root_scale = jnp.sqrt(inverse_norm)
    matrix_full = matrix.astype(f32)
    first = dot_nn(gram_panel, column_panel)
    mixture = (
        cubic_term * root_scale * matrix_full + quintic_term * root_scale * inverse_norm * first
    ).astype(bf16)
    second = dot_nn(gram_panel, lax.all_gather(mixture, "dp", axis=0, tiled=True))
    return linear_term * root_scale * matrix_full + inverse_norm * second


def x_bit(i):
    return (i >> 1) & 1


def y_bit(i):
    return (i >> 2) & 1


def x_pick(i):
    return i ^ 2 ^ x_bit(i)


def y_pick(i):
    return i ^ 4 ^ (x_bit(i) ^ y_bit(i))


ROW_DEVICES = 8
VMEM_LIMIT = 16 << 20
CORE = [(i, i ^ 1) for i in range(ROW_DEVICES)]
TAKE_X = [(x_pick(i), i) for i in range(ROW_DEVICES)]
TAKE_Y = [(y_pick(i), i) for i in range(ROW_DEVICES)]
GIVE_X = [(i, x_pick(i)) for i in range(ROW_DEVICES)]
GIVE_Y = [(i, y_pick(i)) for i in range(ROW_DEVICES)]


def over_dp(value, pairs):
    return lax.ppermute(value, "dp", pairs)


def call(kernel, outs, args, scalars=(), scratch=(), flops=0, streamed=False):
    moved = sum(a.size * a.dtype.itemsize for a in [*args, *outs])
    vmem = pl.BlockSpec(memory_space=pltpu.VMEM)
    return pl.pallas_call(
        kernel,
        out_shape=outs,
        in_specs=[pl.BlockSpec(memory_space=pltpu.SMEM)] * len(scalars) + [vmem] * len(args),
        out_specs=[pl.BlockSpec(memory_space=pl.ANY) if streamed else vmem] * len(outs),
        scratch_shapes=list(scratch),
        compiler_params=pltpu.CompilerParams(vmem_limit_bytes=VMEM_LIMIT),
        cost_estimate=pl.CostEstimate(flops=flops, bytes_accessed=moved, transcendentals=0),
    )(*scalars, *[pltpu.with_memory_space_constraint(a, pltpu.VMEM) for a in args])


def split_rows(total, size, z, kept, pieces):
    rows = kept.shape[1]
    for by in range(size):
        at = pl.multiple_of(lax.rem(z + by, size) * rows, rows)
        piece = total[:, pl.ds(at, rows), :]
        if by:
            pieces[by - 1][...] = piece.astype(bf16)
        else:
            kept[...] = piece


def own_gram_kernel(size, z_ref, core_ref, top, bottom, core_top, core_bottom, kept, *rest):
    pieces, total = rest[:-1], rest[-1]
    for q, (left, right) in enumerate([(top, top), (bottom, bottom), (bottom, top)]):
        total[q] = dot_nt(left[...], right[...])
    for core, (first, second) in enumerate([(core_top, core_bottom), (core_bottom, core_top)]):

        @pl.when(core_ref[0] == core)
        def _():
            total[3] = dot_nt(top[...], first[...])
            total[4] = dot_nt(bottom[...], second[...])

    split_rows(total, size, z_ref[0], kept, pieces)


def stacked(top, bottom):
    return jnp.concatenate([top[...], bottom[...]], axis=0)


def early_gram_kernel(size, z_ref, top, bottom, x_bottom, y_top, kept, *rest):
    pieces, total = rest[:-1], rest[-1]
    half = top.shape[0]
    own = stacked(top, bottom)
    for q, right in ((0, x_bottom), (3, y_top)):
        value = dot_nt(own, right[...])
        total[q], total[q + 1] = value[:half], value[half:]
    total[2] = dot_nt(x_bottom[...], y_top[...])
    split_rows(total, size, z_ref[0], kept, pieces)


def late_gram_kernel(size, z_ref, top, bottom, x_top, x_bottom, y_top, y_bottom, kept, *rest):
    pieces, total = rest[:-1], rest[-1]
    half = top.shape[0]
    own = stacked(top, bottom)
    for q, right in ((0, x_top), (5, y_bottom)):
        value = dot_nt(own, right[...])
        total[q], total[q + 1] = value[:half], value[half:]
    total[2] = dot_nt(x_top[...], y_top[...])
    value = dot_nt(stacked(x_top, x_bottom), y_bottom[...])
    total[3], total[4] = value[:half], value[half:]
    split_rows(total, size, z_ref[0], kept, pieces)


def gram(kernel, shape, size, scalars, halves):
    count, rows, columns = shape
    shape = (count, rows // size, columns)
    outs = [jax.ShapeDtypeStruct(shape, f32)] + [jax.ShapeDtypeStruct(shape, bf16)] * (size - 1)
    return call(
        functools.partial(kernel, size),
        outs,
        halves,
        scalars,
        [pltpu.VMEM((count, rows, columns), f32)],
        2 * count * rows * columns * halves[0].shape[1],
    )


def own_assemble_kernel(size, z_ref, *refs):
    parts, (diagonal, beside) = refs[:-2], refs[-2:]
    z = z_ref[0]
    rows, half = parts[0].shape[1], parts[0].shape[2]
    for by, part in enumerate(parts):
        at = lax.rem(z + size - by, size) * rows
        upper, lower = pl.ds(pl.multiple_of(at, rows), rows), pl.ds(pl.multiple_of(half + at, rows), rows)
        diagonal[upper, :half] = part[0]
        diagonal[lower, half:] = part[1]
        diagonal[lower, :half] = part[2]
        beside[upper, :] = part[3]
        beside[lower, :] = part[4]
    diagonal[:half, half:] = diagonal[half:, :half].T


def own_assemble(z, size, parts):
    half = parts[0].shape[2]
    outs = [jax.ShapeDtypeStruct((2 * half, columns), bf16) for columns in (2 * half, half)]
    return call(functools.partial(own_assemble_kernel, size), outs, parts, [z])


def beside_kernel(core_ref, own, other, out):
    half = own.shape[1]
    for core in range(2):

        @pl.when(core_ref[0] == core)
        def _():
            like, unlike = slice(core * half, (core + 1) * half), slice((1 - core) * half, (2 - core) * half)
            out[:half, like] = own[:half]
            out[half:, unlike] = own[half:]
            out[unlike, :half] = other[:half].T
            out[like, half:] = other[half:].T


def beside_of(core, own, other):
    rows = own.shape[0]
    return call(beside_kernel, [jax.ShapeDtypeStruct((rows, rows), bf16)], [own, other], [core])[0]


def rows_at(z, by, size, rows):
    return pl.multiple_of(lax.rem(z + size - by, size) * rows, rows)


def near_assemble_kernel(size, z_ref, *refs):
    parts, near, wholes = refs[:size], refs[size], refs[size + 1 :]
    count, rows, half = parts[0].shape
    for by, part in enumerate(parts):
        at = rows_at(z_ref[0], by, size, rows)
        lower = pl.multiple_of(half + at, rows)
        near[pl.ds(at, rows), :half] = part[0]
        near[pl.ds(lower, rows), :half] = part[1]
        near[pl.ds(at, rows), half:] = part[count - 2]
        near[pl.ds(lower, rows), half:] = part[count - 1]
        for k, whole in enumerate(wholes):
            whole[:, pl.ds(at, rows), :] = part[2 * k : count - 2 + 2 * k]


def near_assemble(z, size, parts, with_wholes):
    count, _, half = parts[0].shape
    outs = [jax.ShapeDtypeStruct((2 * half, 2 * half), bf16)]
    if with_wholes:
        outs += [jax.ShapeDtypeStruct((count - 2, half, half), bf16)] * 2
    return call(functools.partial(near_assemble_kernel, size), outs, parts, [z])


def shifts_of(size):
    return [by for by in range(1, size) if by * 2 != size], size // 2


def mirror_assemble_kernel(size, z_ref, *refs):
    x_early, y_early, *late, side, linked, crossed, x_late, y_late = refs
    rows, half = late[0].shape[1:]
    packed, last = shifts_of(size)
    for shifts, x_part, y_part in zip(([0], packed, [last]), late[::2], late[1::2]):
        for k, by in enumerate(shifts):
            at = pl.ds(rows_at(z_ref[0], by, size, rows), rows)
            x_late[:, at, :] = x_part[:, k * rows : (k + 1) * rows]
            y_late[:, at, :] = y_part[:, k * rows : (k + 1) * rows]
    columns = [slice(k * half, (k + 1) * half) for k in range(4)]
    top, bottom = columns[0], columns[1]
    for k in range(2):
        side[top, columns[k]] = x_late[k].T
        side[bottom, columns[k]] = x_early[k].T
        side[top, columns[2 + k]] = y_early[1 + k].T
        side[bottom, columns[2 + k]] = y_late[3 + k].T
    linked[top, top] = x_late[2]
    linked[bottom, top] = x_early[2]
    linked[top, bottom] = y_early[0].T
    linked[bottom, bottom] = y_late[2].T
    crossed[top, top] = x_late[3]
    crossed[bottom, top] = x_late[4]
    crossed[top, bottom] = y_late[0].T
    crossed[bottom, bottom] = y_late[1].T


def mirror_assemble(z, size, mirrored):
    count, half = mirrored[-1].shape[0], mirrored[-1].shape[2]
    outs = [jax.ShapeDtypeStruct((2 * half, width * half), bf16) for width in (4, 2, 2)]
    return call(
        functools.partial(mirror_assemble_kernel, size),
        outs,
        mirrored,
        [z],
        [pltpu.VMEM((count, half, half), bf16)] * 2,
    )


def product_kernel(n_grams, n_halves, has_sum, finish, tile, stream, *refs):
    refs = list(refs)
    if stream:
        streamed, held, arrived = refs[-3:]
        refs = refs[:-3] + [held]

        def column_copy(t):
            at = pl.ds(pl.multiple_of(t * tile, tile), tile)
            return pltpu.make_async_copy(held.at[:, at], streamed.at[:, at], arrived.at[t])

    if finish:
        inverse_norm = lax.rsqrt(jnp.sum(refs.pop(0)[...], axis=(0, 1), keepdims=True))
        root_scale = jnp.sqrt(inverse_norm)
        scales = finish(root_scale, inverse_norm)
    grams, refs = refs[:n_grams], refs[n_grams:]
    halves, refs = refs[:n_halves], refs[n_halves:]
    summed = refs.pop(0) if has_sum else None
    own, outs = (refs[:2], refs[2:]) if finish else (None, refs)
    columns = halves[0].shape[1]

    def column_tile(t, carry):
        at = pl.ds(pl.multiple_of(t * tile, tile), tile)
        gram = jnp.concatenate([g[...] for g in grams], axis=1)
        value = dot_nn(gram, jnp.concatenate([h[:, at] for h in halves], axis=0))
        if has_sum:
            value = value + summed[:, at]
        if finish:
            block = jnp.concatenate([own[0][:, at], own[1][:, at]], axis=0)
            value = scales[0] * block.astype(f32) + scales[1] * value
        rows = value.shape[0] // len(outs)
        for k, out in enumerate(outs):
            out[:, at] = value[k * rows : (k + 1) * rows].astype(out.dtype)
        if stream:
            column_copy(t).start()
        return carry

    lax.fori_loop(0, columns // tile, column_tile, 0)
    if stream:

        def wait(t, carry):
            column_copy(t).wait()
            return carry

        lax.fori_loop(0, columns // tile, wait, 0)


def product(grams, halves, summed=None, finish=None, dtype=f32, parts=1):
    half, columns = halves[0].shape
    tile = 256 if columns % 256 == 0 else columns
    args = ([finish[1]] if finish else []) + list(grams) + list(halves)
    args += [] if summed is None else [summed]
    args += list(finish[2]) if finish else []
    outs = [jax.ShapeDtypeStruct((2 * half // parts, columns), dtype)] * parts
    stream = bool(finish) and parts == 1
    return call(
        functools.partial(
            product_kernel, len(grams), len(halves), summed is not None, finish and finish[0], tile, stream
        ),
        outs,
        args,
        scratch=[pltpu.VMEM(outs[0].shape, dtype), pltpu.SemaphoreType.DMA((columns // tile,))] if stream else (),
        streamed=stream,
        flops=4 * half * half * columns * len(halves),
    )


def shifted(value, by, size):
    return lax.ppermute(value, "shard", [(z, (z + by) % size) for z in range(size)])


def total_of(value, size):
    value = sum([shifted(value, by, size) for by in range(1, size)], value)
    for step in (1, 2, 4):
        value = value + over_dp(value, [(i, i ^ step) for i in range(ROW_DEVICES)])
    return value


def gather(block):
    top, bottom = block
    x_bottom, y_top = over_dp(bottom, TAKE_X), over_dp(top, TAKE_Y)
    x_top, y_bottom = over_dp(top, TAKE_X), over_dp(bottom, TAKE_Y)
    core = over_dp(top, CORE), over_dp(bottom, CORE)
    d_oth_bottom, d_sel_top = over_dp(x_bottom, GIVE_Y), over_dp(y_top, GIVE_X)
    x_oth_bottom, y_oth_top = over_dp(x_bottom, CORE), over_dp(y_top, CORE)
    x_oth_top, y_oth_bottom = over_dp(x_top, CORE), over_dp(y_bottom, CORE)
    side = x_oth_top, x_oth_bottom, y_oth_top, y_oth_bottom
    crossed = over_dp(d_oth_bottom, CORE), over_dp(d_sel_top, CORE)
    return core, (x_bottom, y_top), (x_top, y_bottom), side, (d_sel_top, d_oth_bottom), crossed


def fold_kernel(weights, *refs):
    kept, *pieces, before, out, squares = refs
    total = kept[...]
    for piece in pieces:
        total = total + piece[...].astype(f32)
    part = total.astype(bf16)
    out[...] = part
    total = before[...]
    for index, weight in enumerate(weights):
        square = jnp.square(part[index].astype(f32))
        square = sum(square[:, k : k + 128] for k in range(0, square.shape[1], 128))
        total = total + weight * jnp.sum(square.reshape(-1, 8, 128), axis=0)
    squares[...] = total


def reduce_parts(pieces, size, before, weights):
    kept, *sent = pieces
    received = [shifted(piece, by, size) for by, piece in enumerate(sent, 1)]
    outs = [jax.ShapeDtypeStruct(kept.shape, bf16), jax.ShapeDtypeStruct(before.shape, f32)]
    return call(functools.partial(fold_kernel, weights), outs, [kept, *received, before])


def spread(part, size):
    parts = [part]
    for by in range(1, size):
        parts.append(shifted(part, by, size))
    return parts


def iterate_square(matrix, size, gain, dtype, parts):
    z = lax.axis_index("shard").reshape(1)
    side_index = (lax.axis_index("dp") & 1).reshape(1)
    core, one, two, side, linked, crossed = gather(matrix)
    (x_bottom, y_top), (x_top, y_bottom) = one, two
    half = matrix[0].shape[0]
    own_pieces = gram(own_gram_kernel, (5, half, half), size, [z, side_index], [*matrix, *core])
    own_part, squares = reduce_parts(
        own_pieces, size, jnp.zeros((8, 128), f32), (1.0, 1.0, 2.0, 2.0, 2.0)
    )
    own_parts = spread(own_part, size)
    early_pieces = gram(early_gram_kernel, (5, half, half), size, [z], [*matrix, x_bottom, y_top])
    early_part, squares = reduce_parts(early_pieces, size, squares, (2.0,) * 5)
    late_pieces = gram(
        late_gram_kernel, (7, half, half), size, [z], [*matrix, x_top, x_bottom, y_top, y_bottom]
    )
    late_part, squares = reduce_parts(late_pieces, size, squares, (2.0,) * 7)
    squares = total_of(squares, size)
    early_parts = spread(early_part, size)
    late_parts = spread(late_part, size)
    near_one, x_whole, y_whole = near_assemble(z, size, early_parts, True)
    early = over_dp(x_whole, GIVE_X), over_dp(y_whole, GIVE_Y)
    packed, last = shifts_of(size)
    late_own = over_dp(late_part[:-2], GIVE_X), over_dp(late_part[2:], GIVE_Y)
    x_pack = jnp.concatenate([late_parts[by][:-2] for by in packed], axis=1)
    y_pack = jnp.concatenate([late_parts[by][2:] for by in packed], axis=1)
    late_packed = over_dp(x_pack, GIVE_X), over_dp(y_pack, GIVE_Y)
    late_last = over_dp(late_parts[last][:-2], GIVE_X), over_dp(late_parts[last][2:], GIVE_Y)
    own, beside = own_assemble(z, size, own_parts)
    beside = beside_of(side_index, beside, over_dp(beside, CORE))
    (near_two,) = near_assemble(z, size, late_parts, False)
    side_gram, linked_gram, crossed_gram = mirror_assemble(
        z, size, [*early, *late_own, *late_packed, *late_last]
    )

    def mixing(root_scale, inverse_norm):
        return cubic_term * root_scale, quintic_term * root_scale * inverse_norm

    def ending(root_scale, inverse_norm):
        return gain * linear_term * root_scale, gain * inverse_norm

    (first,) = product([own, beside], [*matrix, *core])
    (first,) = product([near_one, near_two], [*one, *two], first)
    mixture = product(
        [side_gram, linked_gram, crossed_gram],
        [*side, *linked, *crossed],
        first,
        (mixing, squares, matrix),
        bf16,
        2,
    )
    core, one, two, side, linked, crossed = gather(mixture)
    (second,) = product([own, beside], [*mixture, *core])
    (second,) = product([near_one], one, second)
    (second,) = product([near_two, side_gram], [*two, *side], second)
    (second,) = product([linked_gram], linked, second)
    return product([crossed_gram], crossed, second, (ending, squares, matrix), dtype, parts)


def current_of(momentum, gradient):
    grad_full = gradient.astype(f32)
    new_momentum = momentum_decay * momentum + grad_full
    return new_momentum, grad_full + momentum_decay * new_momentum


def body_square(size, columns, momentum, gradient):
    half = momentum.shape[0] // 2
    block = [
        current_of(momentum[rows], gradient[rows])[1].astype(bf16)
        for rows in (slice(0, half), slice(half, None))
    ]
    new_momentum, _ = current_of(*lax.optimization_barrier((momentum, gradient)))
    for iteration in range(STEPS):
        last = iteration == STEPS - 1
        block = iterate_square(
            block, size, math.sqrt(columns) if last else 1.0, f32 if last else bf16, 1 if last else 2
        )
    return (new_momentum, block[0])


def body_general(columns, momentum, gradient):
    grad_full = gradient.astype(f32)
    new_momentum = momentum_decay * momentum + grad_full
    current = grad_full + momentum_decay * new_momentum
    for _ in range(STEPS):
        current = iterate_general(current)
    return (new_momentum, math.sqrt(columns) * current)


def solution(mesh):
    row_devices, column_devices = mesh.shape["dp"], mesh.shape["shard"]
    spec = P("dp", "shard")

    def sharded(body):
        return jax.shard_map(body, mesh=mesh, in_specs=(spec, spec), out_specs=(spec, spec), check_vma=False)

    def general(momentum, gradient):
        return sharded(functools.partial(body_general, momentum.shape[1]))(momentum, gradient)

    def square(momentum, gradient):
        return sharded(functools.partial(body_square, column_devices, momentum.shape[1]))(momentum, gradient)

    if row_devices != ROW_DEVICES or column_devices % 4 or column_devices & (column_devices - 1):
        return general
    return square
```

```python
import functools
import math

import jax
import jax.numpy as jnp
from jax import lax
from jax.experimental import pallas as pl
from jax.experimental.pallas import tpu as pltpu
from jax.sharding import PartitionSpec as P


STEPS = 2


momentum_decay = 0.95
linear_term = 3.4445
cubic_term = -4.775
quintic_term = 2.0315

f32, bf16 = jnp.float32, jnp.bfloat16


def dot_nn(a, b):
    return lax.dot_general(a, b, (((1,), (0,)), ((), ())), preferred_element_type=f32)


def dot_nt(a, b):
    return lax.dot_general(a, b, (((1,), (1,)), ((), ())), preferred_element_type=f32)


def iterate_general(current):
    matrix = current.astype(bf16)
    column_panel = lax.all_gather(matrix, "dp", axis=0, tiled=True)
    summed_part = lax.psum_scatter(dot_nt(matrix, column_panel), "shard", scatter_dimension=0, tiled=True)
    gram_part = summed_part.astype(bf16)
    gram_panel = lax.all_gather(gram_part, "shard", axis=0, tiled=True)
    square_sum = lax.psum(jnp.sum(jnp.square(gram_part.astype(f32))), ("dp", "shard"))
    inverse_norm = lax.rsqrt(square_sum)
    root_scale = jnp.sqrt(inverse_norm)
    matrix_full = matrix.astype(f32)
    first = dot_nn(gram_panel, column_panel)
    mixture = (
        cubic_term * root_scale * matrix_full + quintic_term * root_scale * inverse_norm * first
    ).astype(bf16)
    second = dot_nn(gram_panel, lax.all_gather(mixture, "dp", axis=0, tiled=True))
    return linear_term * root_scale * matrix_full + inverse_norm * second


def x_bit(i):
    return (i >> 1) & 1


def y_bit(i):
    return (i >> 2) & 1


def x_pick(i):
    return i ^ 2 ^ x_bit(i)


def y_pick(i):
    return i ^ 4 ^ (x_bit(i) ^ y_bit(i))


ROW_DEVICES = 8
COLUMN_DEVICES = 4
VMEM_LIMIT = 16 << 20
CORE = [(i, i ^ 1) for i in range(ROW_DEVICES)]
TAKE_X = [(x_pick(i), i) for i in range(ROW_DEVICES)]
TAKE_Y = [(y_pick(i), i) for i in range(ROW_DEVICES)]
GIVE_X = [(i, x_pick(i)) for i in range(ROW_DEVICES)]
GIVE_Y = [(i, y_pick(i)) for i in range(ROW_DEVICES)]


def over_dp(value, pairs):
    return lax.ppermute(value, "dp", pairs)


def call(kernel, outs, args, scalars=(), scratch=(), flops=0, streamed=False):
    moved = sum(a.size * a.dtype.itemsize for a in [*args, *outs])
    vmem = pl.BlockSpec(memory_space=pltpu.VMEM)
    return pl.pallas_call(
        kernel,
        out_shape=outs,
        in_specs=[pl.BlockSpec(memory_space=pltpu.SMEM)] * len(scalars) + [vmem] * len(args),
        out_specs=[pl.BlockSpec(memory_space=pl.ANY) if streamed else vmem] * len(outs),
        scratch_shapes=list(scratch),
        compiler_params=pltpu.CompilerParams(vmem_limit_bytes=VMEM_LIMIT),
        cost_estimate=pl.CostEstimate(flops=flops, bytes_accessed=moved, transcendentals=0),
    )(*scalars, *[pltpu.with_memory_space_constraint(a, pltpu.VMEM) for a in args])


def rows_at(z, k, rows):
    return pl.ds(pl.multiple_of((z ^ k) * rows, rows), rows)


def split_rows(total, z, outs):
    rows = outs[0].shape[1]
    for k, out in enumerate(outs):
        out[...] = total[:, rows_at(z, k, rows), :].astype(out.dtype)


def own_gram_kernel(z_ref, core_ref, top, bottom, core_top, core_bottom, *rest):
    outs, total = rest[:-1], rest[-1]
    for q, (left, right) in enumerate([(top, top), (bottom, bottom), (bottom, top)]):
        total[q] = dot_nt(left[...], right[...])
    for core, (first, second) in enumerate([(core_top, core_bottom), (core_bottom, core_top)]):

        @pl.when(core_ref[0] == core)
        def _():
            total[3] = dot_nt(top[...], first[...])
            total[4] = dot_nt(bottom[...], second[...])

    split_rows(total, z_ref[0], outs)


def stacked(top, bottom):
    return jnp.concatenate([top[...], bottom[...]], axis=0)


def early_gram_kernel(z_ref, top, bottom, x_bottom, y_top, *rest):
    outs, total = rest[:-1], rest[-1]
    half = top.shape[0]
    own = stacked(top, bottom)
    for q, right in ((0, x_bottom), (3, y_top)):
        value = dot_nt(own, right[...])
        total[q], total[q + 1] = value[:half], value[half:]
    total[2] = dot_nt(x_bottom[...], y_top[...])
    split_rows(total, z_ref[0], outs)


def late_gram_kernel(z_ref, top, bottom, x_top, x_bottom, y_top, y_bottom, *rest):
    outs, total = rest[:-1], rest[-1]
    half = top.shape[0]
    own = stacked(top, bottom)
    for q, right in ((0, x_top), (5, y_bottom)):
        value = dot_nt(own, right[...])
        total[q], total[q + 1] = value[:half], value[half:]
    total[2] = dot_nt(x_top[...], y_top[...])
    value = dot_nt(stacked(x_top, x_bottom), y_bottom[...])
    total[3], total[4] = value[:half], value[half:]
    split_rows(total, z_ref[0], outs)


def gram(kernel, shape, scalars, halves):
    count, rows, columns = shape
    shape = (count, rows // COLUMN_DEVICES, columns)
    return call(
        kernel,
        [jax.ShapeDtypeStruct(shape, kind) for kind in (f32, bf16, f32, bf16)],
        halves,
        scalars,
        [pltpu.VMEM((count, rows, columns), f32)],
        2 * count * rows * columns * halves[0].shape[1],
    )


def own_assemble_kernel(z_ref, *refs):
    parts, (diagonal, beside) = refs[:-2], refs[-2:]
    rows, half = parts[0].shape[1:]
    for k, part in enumerate(parts):
        at = rows_at(z_ref[0], k, rows)
        lower = pl.ds(pl.multiple_of(half + at.start, rows), rows)
        diagonal[at, :half] = part[0]
        diagonal[lower, half:] = part[1]
        diagonal[lower, :half] = part[2]
        beside[at, :] = part[3]
        beside[lower, :] = part[4]
    diagonal[:half, half:] = diagonal[half:, :half].T


def own_assemble(z, parts):
    half = parts[0].shape[2]
    outs = [jax.ShapeDtypeStruct((2 * half, columns), bf16) for columns in (2 * half, half)]
    return call(own_assemble_kernel, outs, parts, [z])


def beside_kernel(core_ref, own, other, out):
    half = own.shape[1]
    for core in range(2):

        @pl.when(core_ref[0] == core)
        def _():
            like, unlike = slice(core * half, (core + 1) * half), slice((1 - core) * half, (2 - core) * half)
            out[:half, like] = own[:half]
            out[half:, unlike] = own[half:]
            out[unlike, :half] = other[:half].T
            out[like, half:] = other[half:].T


def beside_of(core, own, other):
    rows = own.shape[0]
    return call(beside_kernel, [jax.ShapeDtypeStruct((rows, rows), bf16)], [own, other], [core])[0]


def near_assemble_kernel(z_ref, *refs):
    parts, near, wholes = refs[:COLUMN_DEVICES], refs[COLUMN_DEVICES], refs[COLUMN_DEVICES + 1 :]
    count, rows, half = parts[0].shape
    for k, part in enumerate(parts):
        at = rows_at(z_ref[0], k, rows)
        lower = pl.ds(pl.multiple_of(half + at.start, rows), rows)
        near[at, :half] = part[0]
        near[lower, :half] = part[1]
        near[at, half:] = part[count - 2]
        near[lower, half:] = part[count - 1]
        for w, whole in enumerate(wholes):
            whole[:, at, :] = part[2 * w : count - 2 + 2 * w]


def near_assemble(z, parts, with_wholes):
    count, _, half = parts[0].shape
    outs = [jax.ShapeDtypeStruct((2 * half, 2 * half), bf16)]
    if with_wholes:
        outs += [jax.ShapeDtypeStruct((count - 2, half, half), bf16)] * 2
    return call(near_assemble_kernel, outs, parts, [z])


def mirror_assemble_kernel(z_ref, *refs):
    x_early, y_early, *late, side, linked, crossed, x_late, y_late = refs
    rows, half = late[0].shape[1:]
    for shifts, x_part, y_part in zip(((0,), (1, 2), (3,)), late[::2], late[1::2]):
        for k, shift in enumerate(shifts):
            at = rows_at(z_ref[0], shift, rows)
            x_late[:, at, :] = x_part[:, k * rows : (k + 1) * rows]
            y_late[:, at, :] = y_part[:, k * rows : (k + 1) * rows]
    columns = [slice(k * half, (k + 1) * half) for k in range(4)]
    top, bottom = columns[0], columns[1]
    for k in range(2):
        side[top, columns[k]] = x_late[k].T
        side[bottom, columns[k]] = x_early[k].T
        side[top, columns[2 + k]] = y_early[1 + k].T
        side[bottom, columns[2 + k]] = y_late[3 + k].T
    linked[top, top] = x_late[2]
    linked[bottom, top] = x_early[2]
    linked[top, bottom] = y_early[0].T
    linked[bottom, bottom] = y_late[2].T
    crossed[top, top] = x_late[3]
    crossed[bottom, top] = x_late[4]
    crossed[top, bottom] = y_late[0].T
    crossed[bottom, bottom] = y_late[1].T


def mirror_assemble(z, mirrored):
    count, _, half = mirrored[-1].shape
    outs = [jax.ShapeDtypeStruct((2 * half, width * half), bf16) for width in (4, 2, 2)]
    return call(mirror_assemble_kernel, outs, mirrored, [z], [pltpu.VMEM((count, half, half), bf16)] * 2)


def product_kernel(n_grams, n_halves, has_sum, finish, tile, stream, *refs):
    refs = list(refs)
    if stream:
        streamed, held, arrived = refs[-3:]
        refs = refs[:-3] + [held]

        def column_copy(t):
            at = pl.ds(pl.multiple_of(t * tile, tile), tile)
            return pltpu.make_async_copy(held.at[:, at], streamed.at[:, at], arrived.at[t])

    if finish:
        inverse_norm = lax.rsqrt(jnp.sum(refs.pop(0)[...], axis=(0, 1), keepdims=True))
        root_scale = jnp.sqrt(inverse_norm)
        scales = finish(root_scale, inverse_norm)
    grams, refs = refs[:n_grams], refs[n_grams:]
    halves, refs = refs[:n_halves], refs[n_halves:]
    summed = refs.pop(0) if has_sum else None
    own, outs = (refs[:2], refs[2:]) if finish else (None, refs)
    columns = halves[0].shape[1]

    def column_tile(t, carry):
        at = pl.ds(pl.multiple_of(t * tile, tile), tile)
        gram = jnp.concatenate([g[...] for g in grams], axis=1)
        value = dot_nn(gram, jnp.concatenate([h[:, at] for h in halves], axis=0))
        if has_sum:
            value = value + summed[:, at]
        if finish:
            block = jnp.concatenate([own[0][:, at], own[1][:, at]], axis=0)
            value = scales[0] * block.astype(f32) + scales[1] * value
        rows = value.shape[0] // len(outs)
        for k, out in enumerate(outs):
            out[:, at] = value[k * rows : (k + 1) * rows].astype(out.dtype)
        if stream:
            column_copy(t).start()
        return carry

    lax.fori_loop(0, columns // tile, column_tile, 0)
    if stream:

        def wait(t, carry):
            column_copy(t).wait()
            return carry

        lax.fori_loop(0, columns // tile, wait, 0)


def product(grams, halves, summed=None, finish=None, dtype=f32, parts=1):
    half, columns = halves[0].shape
    tile = 256 if columns % 256 == 0 else columns
    args = ([finish[1]] if finish else []) + list(grams) + list(halves)
    args += [] if summed is None else [summed]
    args += list(finish[2]) if finish else []
    outs = [jax.ShapeDtypeStruct((2 * half // parts, columns), dtype)] * parts
    stream = bool(finish) and parts == 1
    return call(
        functools.partial(
            product_kernel, len(grams), len(halves), summed is not None, finish and finish[0], tile, stream
        ),
        outs,
        args,
        scratch=[pltpu.VMEM(outs[0].shape, dtype), pltpu.SemaphoreType.DMA((columns // tile,))] if stream else (),
        streamed=stream,
        flops=4 * half * half * columns * len(halves),
    )


def exchanged(value, distance):
    return lax.ppermute(value, "shard", [(z, z ^ distance) for z in range(COLUMN_DEVICES)])


def total_of(value):
    value = value + exchanged(value, 1) + (exchanged(value, 2) + exchanged(value, 3))
    for step in (1, 2, 4):
        value = value + over_dp(value, [(i, i ^ step) for i in range(ROW_DEVICES)])
    return value


def gather(block):
    top, bottom = block
    x_bottom, y_top = over_dp(bottom, TAKE_X), over_dp(top, TAKE_Y)
    x_top, y_bottom = over_dp(top, TAKE_X), over_dp(bottom, TAKE_Y)
    core = over_dp(top, CORE), over_dp(bottom, CORE)
    d_oth_bottom, d_sel_top = over_dp(x_bottom, GIVE_Y), over_dp(y_top, GIVE_X)
    x_oth_bottom, y_oth_top = over_dp(x_bottom, CORE), over_dp(y_top, CORE)
    x_oth_top, y_oth_bottom = over_dp(x_top, CORE), over_dp(y_bottom, CORE)
    side = x_oth_top, x_oth_bottom, y_oth_top, y_oth_bottom
    crossed = over_dp(d_oth_bottom, CORE), over_dp(d_sel_top, CORE)
    return core, (x_bottom, y_top), (x_top, y_bottom), side, (d_sel_top, d_oth_bottom), crossed


def add_kernel(kept, piece, out):
    out[...] = (kept[...] + piece[...].astype(f32)).astype(out.dtype)


def fold_kernel(weights, *refs):
    kept, *pieces, before, out, squares = refs
    total = kept[...]
    for piece in pieces:
        total = total + piece[...].astype(f32)
    part = total.astype(bf16)
    out[...] = part
    total = before[...]
    for index, weight in enumerate(weights):
        square = jnp.square(part[index].astype(f32))
        square = sum(square[:, k : k + 128] for k in range(0, square.shape[1], 128))
        total = total + weight * jnp.sum(square.reshape(-1, 8, 128), axis=0)
    squares[...] = total


def reduce_parts(pieces, before, weights):
    kept, one, passed, three = pieces
    three, one = exchanged(three, 1), exchanged(one, 1)
    out = jax.ShapeDtypeStruct(kept.shape, bf16)
    (two,) = call(add_kernel, [out], [passed, three])
    two = exchanged(two, 2)
    outs = [out, jax.ShapeDtypeStruct(before.shape, f32)]
    return call(functools.partial(fold_kernel, weights), outs, [kept, one, two, before])


def spread(part):
    two, one = exchanged(part, 2), exchanged(part, 1)
    three = exchanged(two, 1)
    return [part, one, two, three]


def iterate_square(matrix, gain, dtype, parts):
    z = lax.axis_index("shard").reshape(1)
    side_index = (lax.axis_index("dp") & 1).reshape(1)
    core, one, two, side, linked, crossed = gather(matrix)
    (x_bottom, y_top), (x_top, y_bottom) = one, two
    half = matrix[0].shape[0]
    own_pieces = gram(own_gram_kernel, (5, half, half), [z, side_index], [*matrix, *core])
    own_part, squares = reduce_parts(own_pieces, jnp.zeros((8, 128), f32), (1.0, 1.0, 2.0, 2.0, 2.0))
    own_parts = spread(own_part)
    early_pieces = gram(early_gram_kernel, (5, half, half), [z], [*matrix, x_bottom, y_top])
    early_part, squares = reduce_parts(early_pieces, squares, (2.0,) * 5)
    late_pieces = gram(
        late_gram_kernel, (7, half, half), [z], [*matrix, x_top, x_bottom, y_top, y_bottom]
    )
    late_part, squares = reduce_parts(late_pieces, squares, (2.0,) * 7)
    squares = total_of(squares)
    early_parts = spread(early_part)
    late_parts = spread(late_part)
    near_one, x_whole, y_whole = near_assemble(z, early_parts, True)
    early = over_dp(x_whole, GIVE_X), over_dp(y_whole, GIVE_Y)
    late = []
    for shifts in ((0,), (1, 2), (3,)):
        x_part, y_part = late_parts[shifts[0]][:-2], late_parts[shifts[0]][2:]
        if len(shifts) > 1:
            x_part = jnp.concatenate([late_parts[k][:-2] for k in shifts], axis=1)
            y_part = jnp.concatenate([late_parts[k][2:] for k in shifts], axis=1)
        late += [over_dp(x_part, GIVE_X), over_dp(y_part, GIVE_Y)]
    own, beside = own_assemble(z, own_parts)
    beside = beside_of(side_index, beside, over_dp(beside, CORE))
    (near_two,) = near_assemble(z, late_parts, False)
    side_gram, linked_gram, crossed_gram = mirror_assemble(z, [*early, *late])

    def mixing(root_scale, inverse_norm):
        return cubic_term * root_scale, quintic_term * root_scale * inverse_norm

    def ending(root_scale, inverse_norm):
        return gain * linear_term * root_scale, gain * inverse_norm

    (first,) = product([own, beside], [*matrix, *core])
    (first,) = product([near_one, near_two], [*one, *two], first)
    mixture = product(
        [side_gram, linked_gram, crossed_gram],
        [*side, *linked, *crossed],
        first,
        (mixing, squares, matrix),
        bf16,
        2,
    )
    core, one, two, side, linked, crossed = gather(mixture)
    (second,) = product([own, beside], [*mixture, *core])
    (second,) = product([near_one], one, second)
    (second,) = product([near_two, side_gram], [*two, *side], second)
    (second,) = product([linked_gram], linked, second)
    return product([crossed_gram], crossed, second, (ending, squares, matrix), dtype, parts)


def current_of(momentum, gradient):
    grad_full = gradient.astype(f32)
    new_momentum = momentum_decay * momentum + grad_full
    return new_momentum, grad_full + momentum_decay * new_momentum


def body_square(columns, momentum, gradient):
    half = momentum.shape[0] // 2
    block = [
        current_of(momentum[rows], gradient[rows])[1].astype(bf16)
        for rows in (slice(0, half), slice(half, None))
    ]
    new_momentum, _ = current_of(*lax.optimization_barrier((momentum, gradient)))
    for iteration in range(STEPS):
        last = iteration == STEPS - 1
        block = iterate_square(
            block, math.sqrt(columns) if last else 1.0, f32 if last else bf16, 1 if last else 2
        )
    return (new_momentum, block[0])


def body_general(columns, momentum, gradient):
    grad_full = gradient.astype(f32)
    new_momentum = momentum_decay * momentum + grad_full
    current = grad_full + momentum_decay * new_momentum
    for _ in range(STEPS):
        current = iterate_general(current)
    return (new_momentum, math.sqrt(columns) * current)


def solution(mesh):
    row_devices, column_devices = mesh.shape["dp"], mesh.shape["shard"]
    spec = P("dp", "shard")

    def sharded(body):
        return jax.shard_map(body, mesh=mesh, in_specs=(spec, spec), out_specs=(spec, spec), check_vma=False)

    def general(momentum, gradient):
        return sharded(functools.partial(body_general, momentum.shape[1]))(momentum, gradient)

    def square(momentum, gradient):
        return sharded(functools.partial(body_square, momentum.shape[1]))(momentum, gradient)

    if (row_devices, column_devices) != (ROW_DEVICES, COLUMN_DEVICES):
        return general
    return square
```

```python
import functools
import math

import jax
import jax.numpy as jnp
from jax import lax
from jax.experimental import pallas as pl
from jax.experimental.pallas import tpu as pltpu
from jax.sharding import PartitionSpec as P


STEPS = 2


momentum_decay = 0.95
linear_term = 3.4445
cubic_term = -4.775
quintic_term = 2.0315

f32, bf16 = jnp.float32, jnp.bfloat16


def dot_nn(a, b):
    return lax.dot_general(a, b, (((1,), (0,)), ((), ())), preferred_element_type=f32)


def dot_nt(a, b):
    return lax.dot_general(a, b, (((1,), (1,)), ((), ())), preferred_element_type=f32)


def iterate_general(current):
    matrix = current.astype(bf16)
    column_panel = lax.all_gather(matrix, "dp", axis=0, tiled=True)
    summed_part = lax.psum_scatter(dot_nt(matrix, column_panel), "shard", scatter_dimension=0, tiled=True)
    gram_part = summed_part.astype(bf16)
    gram_panel = lax.all_gather(gram_part, "shard", axis=0, tiled=True)
    square_sum = lax.psum(jnp.sum(jnp.square(gram_part.astype(f32))), ("dp", "shard"))
    inverse_norm = lax.rsqrt(square_sum)
    root_scale = jnp.sqrt(inverse_norm)
    matrix_full = matrix.astype(f32)
    first = dot_nn(gram_panel, column_panel)
    mixture = (
        cubic_term * root_scale * matrix_full + quintic_term * root_scale * inverse_norm * first
    ).astype(bf16)
    second = dot_nn(gram_panel, lax.all_gather(mixture, "dp", axis=0, tiled=True))
    return linear_term * root_scale * matrix_full + inverse_norm * second


def x_bit(i):
    return (i >> 1) & 1


def y_bit(i):
    return (i >> 2) & 1


def x_pick(i):
    return i ^ 2 ^ x_bit(i)


def y_pick(i):
    return i ^ 4 ^ (x_bit(i) ^ y_bit(i))


ROW_DEVICES = 8
COLUMN_DEVICES = 4
VMEM_LIMIT = 16 << 20
CORE = [(i, i ^ 1) for i in range(ROW_DEVICES)]
TAKE_X = [(x_pick(i), i) for i in range(ROW_DEVICES)]
TAKE_Y = [(y_pick(i), i) for i in range(ROW_DEVICES)]
GIVE_X = [(i, x_pick(i)) for i in range(ROW_DEVICES)]
GIVE_Y = [(i, y_pick(i)) for i in range(ROW_DEVICES)]


def over_dp(value, pairs):
    return lax.ppermute(value, "dp", pairs)


def call(kernel, outs, args, scalars=(), scratch=(), flops=0, streamed=False):
    moved = sum(a.size * a.dtype.itemsize for a in [*args, *outs])
    vmem = pl.BlockSpec(memory_space=pltpu.VMEM)
    return pl.pallas_call(
        kernel,
        out_shape=outs,
        in_specs=[pl.BlockSpec(memory_space=pltpu.SMEM)] * len(scalars) + [vmem] * len(args),
        out_specs=[pl.BlockSpec(memory_space=pl.ANY) if streamed else vmem] * len(outs),
        scratch_shapes=list(scratch),
        compiler_params=pltpu.CompilerParams(vmem_limit_bytes=VMEM_LIMIT),
        cost_estimate=pl.CostEstimate(flops=flops, bytes_accessed=moved, transcendentals=0),
    )(*scalars, *[pltpu.with_memory_space_constraint(a, pltpu.VMEM) for a in args])


def rows_at(z, k, rows):
    return pl.ds(pl.multiple_of((z ^ k) * rows, rows), rows)


def split_rows(total, z, outs):
    rows = outs[0].shape[1]
    for k, out in enumerate(outs):
        out[...] = total[:, rows_at(z, k, rows), :].astype(out.dtype)


def own_gram_kernel(z_ref, core_ref, top, bottom, core_top, core_bottom, *rest):
    outs, total = rest[:-1], rest[-1]
    for q, (left, right) in enumerate([(top, top), (bottom, bottom), (bottom, top)]):
        total[q] = dot_nt(left[...], right[...])
    for core, (first, second) in enumerate([(core_top, core_bottom), (core_bottom, core_top)]):

        @pl.when(core_ref[0] == core)
        def _():
            total[3] = dot_nt(top[...], first[...])
            total[4] = dot_nt(bottom[...], second[...])

    split_rows(total, z_ref[0], outs)


def stacked(top, bottom):
    return jnp.concatenate([top[...], bottom[...]], axis=0)


def early_gram_kernel(z_ref, top, bottom, x_bottom, y_top, *rest):
    outs, total = rest[:-1], rest[-1]
    half = top.shape[0]
    own = stacked(top, bottom)
    for q, right in ((0, x_bottom), (3, y_top)):
        value = dot_nt(own, right[...])
        total[q], total[q + 1] = value[:half], value[half:]
    total[2] = dot_nt(x_bottom[...], y_top[...])
    split_rows(total, z_ref[0], outs)


def late_gram_kernel(z_ref, top, bottom, x_top, x_bottom, y_top, y_bottom, *rest):
    outs, total = rest[:-1], rest[-1]
    half = top.shape[0]
    own = stacked(top, bottom)
    for q, right in ((0, x_top), (5, y_bottom)):
        value = dot_nt(own, right[...])
        total[q], total[q + 1] = value[:half], value[half:]
    total[2] = dot_nt(x_top[...], y_top[...])
    value = dot_nt(stacked(x_top, x_bottom), y_bottom[...])
    total[3], total[4] = value[:half], value[half:]
    split_rows(total, z_ref[0], outs)


def gram(kernel, shape, scalars, halves):
    count, rows, columns = shape
    shape = (count, rows // COLUMN_DEVICES, columns)
    return call(
        kernel,
        [jax.ShapeDtypeStruct(shape, kind) for kind in (f32, bf16, f32, bf16)],
        halves,
        scalars,
        [pltpu.VMEM((count, rows, columns), f32)],
        2 * count * rows * columns * halves[0].shape[1],
    )


def own_assemble_kernel(z_ref, *refs):
    parts, (diagonal, beside) = refs[:-2], refs[-2:]
    rows, half = parts[0].shape[1:]
    for k, part in enumerate(parts):
        at = rows_at(z_ref[0], k, rows)
        lower = pl.ds(pl.multiple_of(half + at.start, rows), rows)
        diagonal[at, :half] = part[0]
        diagonal[lower, half:] = part[1]
        diagonal[lower, :half] = part[2]
        beside[at, :] = part[3]
        beside[lower, :] = part[4]
    diagonal[:half, half:] = diagonal[half:, :half].T


def own_assemble(z, parts):
    half = parts[0].shape[2]
    outs = [jax.ShapeDtypeStruct((2 * half, columns), bf16) for columns in (2 * half, half)]
    return call(own_assemble_kernel, outs, parts, [z])


def beside_kernel(core_ref, own, other, out):
    half = own.shape[1]
    for core in range(2):

        @pl.when(core_ref[0] == core)
        def _():
            like, unlike = slice(core * half, (core + 1) * half), slice((1 - core) * half, (2 - core) * half)
            out[:half, like] = own[:half]
            out[half:, unlike] = own[half:]
            out[unlike, :half] = other[:half].T
            out[like, half:] = other[half:].T


def beside_of(core, own, other):
    rows = own.shape[0]
    return call(beside_kernel, [jax.ShapeDtypeStruct((rows, rows), bf16)], [own, other], [core])[0]


def near_assemble_kernel(z_ref, *refs):
    parts, near, wholes = refs[:COLUMN_DEVICES], refs[COLUMN_DEVICES], refs[COLUMN_DEVICES + 1 :]
    count, rows, half = parts[0].shape
    for k, part in enumerate(parts):
        at = rows_at(z_ref[0], k, rows)
        lower = pl.ds(pl.multiple_of(half + at.start, rows), rows)
        near[at, :half] = part[0]
        near[lower, :half] = part[1]
        near[at, half:] = part[count - 2]
        near[lower, half:] = part[count - 1]
        for w, whole in enumerate(wholes):
            whole[:, at, :] = part[2 * w : count - 2 + 2 * w]


def near_assemble(z, parts, with_wholes):
    count, _, half = parts[0].shape
    outs = [jax.ShapeDtypeStruct((2 * half, 2 * half), bf16)]
    if with_wholes:
        outs += [jax.ShapeDtypeStruct((count - 2, half, half), bf16)] * 2
    return call(near_assemble_kernel, outs, parts, [z])


def mirror_assemble_kernel(z_ref, *refs):
    x_early, y_early, *late, side, linked, crossed, x_late, y_late = refs
    rows, half = late[0].shape[1:]
    for shifts, x_part, y_part in zip(((0,), (1, 2), (3,)), late[::2], late[1::2]):
        for k, shift in enumerate(shifts):
            at = rows_at(z_ref[0], shift, rows)
            x_late[:, at, :] = x_part[:, k * rows : (k + 1) * rows]
            y_late[:, at, :] = y_part[:, k * rows : (k + 1) * rows]
    columns = [slice(k * half, (k + 1) * half) for k in range(4)]
    top, bottom = columns[0], columns[1]
    for k in range(2):
        side[top, columns[k]] = x_late[k].T
        side[bottom, columns[k]] = x_early[k].T
        side[top, columns[2 + k]] = y_early[1 + k].T
        side[bottom, columns[2 + k]] = y_late[3 + k].T
    linked[top, top] = x_late[2]
    linked[bottom, top] = x_early[2]
    linked[top, bottom] = y_early[0].T
    linked[bottom, bottom] = y_late[2].T
    crossed[top, top] = x_late[3]
    crossed[bottom, top] = x_late[4]
    crossed[top, bottom] = y_late[0].T
    crossed[bottom, bottom] = y_late[1].T


def mirror_assemble(z, mirrored):
    count, _, half = mirrored[-1].shape
    outs = [jax.ShapeDtypeStruct((2 * half, width * half), bf16) for width in (4, 2, 2)]
    return call(mirror_assemble_kernel, outs, mirrored, [z], [pltpu.VMEM((count, half, half), bf16)] * 2)


def product_kernel(n_grams, n_halves, has_sum, finish, tile, stream, *refs):
    refs = list(refs)
    if stream:
        streamed, held, arrived = refs[-3:]
        refs = refs[:-3] + [held]

        def column_copy(t):
            at = pl.ds(pl.multiple_of(t * tile, tile), tile)
            return pltpu.make_async_copy(held.at[:, at], streamed.at[:, at], arrived.at[t])

    if finish:
        inverse_norm = lax.rsqrt(jnp.sum(refs.pop(0)[...], axis=(0, 1), keepdims=True))
        root_scale = jnp.sqrt(inverse_norm)
        scales = finish(root_scale, inverse_norm)
    grams, refs = refs[:n_grams], refs[n_grams:]
    halves, refs = refs[:n_halves], refs[n_halves:]
    summed = refs.pop(0) if has_sum else None
    own, outs = (refs[:2], refs[2:]) if finish else (None, refs)
    columns = halves[0].shape[1]

    def column_tile(t, carry):
        at = pl.ds(pl.multiple_of(t * tile, tile), tile)
        gram = jnp.concatenate([g[...] for g in grams], axis=1)
        value = dot_nn(gram, jnp.concatenate([h[:, at] for h in halves], axis=0))
        if has_sum:
            value = value + summed[:, at]
        if finish:
            block = jnp.concatenate([own[0][:, at], own[1][:, at]], axis=0)
            value = scales[0] * block.astype(f32) + scales[1] * value
        rows = value.shape[0] // len(outs)
        for k, out in enumerate(outs):
            out[:, at] = value[k * rows : (k + 1) * rows].astype(out.dtype)
        if stream:
            column_copy(t).start()
        return carry

    lax.fori_loop(0, columns // tile, column_tile, 0)
    if stream:

        def wait(t, carry):
            column_copy(t).wait()
            return carry

        lax.fori_loop(0, columns // tile, wait, 0)


def product(grams, halves, summed=None, finish=None, dtype=f32, parts=1):
    half, columns = halves[0].shape
    tile = 256 if columns % 256 == 0 else columns
    args = ([finish[1]] if finish else []) + list(grams) + list(halves)
    args += [] if summed is None else [summed]
    args += list(finish[2]) if finish else []
    outs = [jax.ShapeDtypeStruct((2 * half // parts, columns), dtype)] * parts
    stream = bool(finish) and parts == 1
    return call(
        functools.partial(
            product_kernel, len(grams), len(halves), summed is not None, finish and finish[0], tile, stream
        ),
        outs,
        args,
        scratch=[pltpu.VMEM(outs[0].shape, dtype), pltpu.SemaphoreType.DMA((columns // tile,))] if stream else (),
        streamed=stream,
        flops=4 * half * half * columns * len(halves),
    )


def exchanged(value, distance):
    return lax.ppermute(value, "shard", [(z, z ^ distance) for z in range(COLUMN_DEVICES)])


def total_of(value):
    value = value + over_dp(value, CORE)
    x_side, y_side, diagonal = (over_dp(value, [(i, i ^ k) for i in range(ROW_DEVICES)]) for k in (2, 4, 6))
    return (value + x_side) + (y_side + diagonal)


def gather(block):
    top, bottom = block
    x_bottom, y_top = over_dp(bottom, TAKE_X), over_dp(top, TAKE_Y)
    x_top, y_bottom = over_dp(top, TAKE_X), over_dp(bottom, TAKE_Y)
    core = over_dp(top, CORE), over_dp(bottom, CORE)
    d_oth_bottom, d_sel_top = over_dp(x_bottom, GIVE_Y), over_dp(y_top, GIVE_X)
    x_oth_bottom, y_oth_top = over_dp(x_bottom, CORE), over_dp(y_top, CORE)
    x_oth_top, y_oth_bottom = over_dp(x_top, CORE), over_dp(y_bottom, CORE)
    side = x_oth_top, x_oth_bottom, y_oth_top, y_oth_bottom
    crossed = over_dp(d_oth_bottom, CORE), over_dp(d_sel_top, CORE)
    return core, (x_bottom, y_top), (x_top, y_bottom), side, (d_sel_top, d_oth_bottom), crossed


def add_kernel(kept, *refs):
    total = kept[...]
    for piece in refs[:-1]:
        total = total + piece[...].astype(f32)
    refs[-1][...] = total.astype(bf16)


def reduce_parts(pieces):
    kept, one, passed, three = pieces
    three, one = exchanged(three, 1), exchanged(one, 1)
    out = jax.ShapeDtypeStruct(kept.shape, bf16)
    (two,) = call(add_kernel, [out], [passed, three])
    two = exchanged(two, 2)
    return call(add_kernel, [out], [kept, one, two])[0]


def squares_kernel(weights, *refs):
    *parts, before, out = refs
    total = before[...]
    for part, part_weights in zip(parts, weights):
        for weight in sorted(set(part_weights)):
            square = sum(jnp.square(part[q].astype(f32)) for q, w in enumerate(part_weights) if w == weight)
            square = sum(square[:, k : k + 128] for k in range(0, square.shape[1], 128))
            total = total + weight * jnp.sum(square.reshape(-1, 8, 128), axis=0)
    out[...] = total


def squares_of(parts, weights, before):
    out = jax.ShapeDtypeStruct(before.shape, f32)
    return call(functools.partial(squares_kernel, weights), [out], [*parts, before])[0]


def spread(part):
    two, one = exchanged(part, 2), exchanged(part, 1)
    three = exchanged(two, 1)
    return [part, one, two, three]


def iterate_square(matrix, gain, dtype, parts):
    z = lax.axis_index("shard").reshape(1)
    side_index = (lax.axis_index("dp") & 1).reshape(1)
    core, one, two, side, linked, crossed = gather(matrix)
    (x_bottom, y_top), (x_top, y_bottom) = one, two
    half = matrix[0].shape[0]
    own_pieces = gram(own_gram_kernel, (5, half, half), [z, side_index], [*matrix, *core])
    own_part = reduce_parts(own_pieces)
    own_parts = spread(own_part)
    early_pieces = gram(early_gram_kernel, (5, half, half), [z], [*matrix, x_bottom, y_top])
    early_part = reduce_parts(early_pieces)
    late_pieces = gram(
        late_gram_kernel, (7, half, half), [z], [*matrix, x_top, x_bottom, y_top, y_bottom]
    )
    late_part = reduce_parts(late_pieces)
    early_parts = spread(early_part)
    late_parts = spread(late_part)
    weights = [(1.0, 1.0, 2.0, 2.0, 2.0)] * 4 + [(2.0,) * 5] * 4 + [(2.0,) * 7] * 3
    squares = squares_of([*own_parts, *early_parts, *late_parts[:3]], weights, jnp.zeros((8, 128), f32))
    squares = squares_of(late_parts[3:], [(2.0,) * 7], squares)
    squares = total_of(squares)
    near_one, x_whole, y_whole = near_assemble(z, early_parts, True)
    early = over_dp(x_whole, GIVE_X), over_dp(y_whole, GIVE_Y)
    late = []
    for shifts in ((0,), (1, 2), (3,)):
        x_part, y_part = late_parts[shifts[0]][:-2], late_parts[shifts[0]][2:]
        if len(shifts) > 1:
            x_part = jnp.concatenate([late_parts[k][:-2] for k in shifts], axis=1)
            y_part = jnp.concatenate([late_parts[k][2:] for k in shifts], axis=1)
        late += [over_dp(x_part, GIVE_X), over_dp(y_part, GIVE_Y)]
    own, beside = own_assemble(z, own_parts)
    beside = beside_of(side_index, beside, over_dp(beside, CORE))
    (near_two,) = near_assemble(z, late_parts, False)
    side_gram, linked_gram, crossed_gram = mirror_assemble(z, [*early, *late])

    def mixing(root_scale, inverse_norm):
        return cubic_term * root_scale, quintic_term * root_scale * inverse_norm

    def ending(root_scale, inverse_norm):
        return gain * linear_term * root_scale, gain * inverse_norm

    (first,) = product([own, beside], [*matrix, *core])
    (first,) = product([near_one, near_two], [*one, *two], first)
    mixture = product(
        [side_gram, linked_gram, crossed_gram],
        [*side, *linked, *crossed],
        first,
        (mixing, squares, matrix),
        bf16,
        2,
    )
    core, one, two, side, linked, crossed = gather(mixture)
    (second,) = product([own, beside], [*mixture, *core])
    (second,) = product([near_one], one, second)
    (second,) = product([near_two, side_gram], [*two, *side], second)
    (second,) = product([linked_gram], linked, second)
    return product([crossed_gram], crossed, second, (ending, squares, matrix), dtype, parts)


def current_of(momentum, gradient):
    grad_full = gradient.astype(f32)
    new_momentum = momentum_decay * momentum + grad_full
    return new_momentum, grad_full + momentum_decay * new_momentum


def body_square(columns, momentum, gradient):
    half = momentum.shape[0] // 2
    block = [
        current_of(momentum[rows], gradient[rows])[1].astype(bf16)
        for rows in (slice(0, half), slice(half, None))
    ]
    new_momentum, _ = current_of(*lax.optimization_barrier((momentum, gradient)))
    for iteration in range(STEPS):
        last = iteration == STEPS - 1
        block = iterate_square(
            block, math.sqrt(columns) if last else 1.0, f32 if last else bf16, 1 if last else 2
        )
    return (new_momentum, block[0])


def body_general(columns, momentum, gradient):
    grad_full = gradient.astype(f32)
    new_momentum = momentum_decay * momentum + grad_full
    current = grad_full + momentum_decay * new_momentum
    for _ in range(STEPS):
        current = iterate_general(current)
    return (new_momentum, math.sqrt(columns) * current)


def solution(mesh):
    row_devices, column_devices = mesh.shape["dp"], mesh.shape["shard"]
    spec = P("dp", "shard")

    def sharded(body):
        return jax.shard_map(body, mesh=mesh, in_specs=(spec, spec), out_specs=(spec, spec), check_vma=False)

    def general(momentum, gradient):
        return sharded(functools.partial(body_general, momentum.shape[1]))(momentum, gradient)

    def square(momentum, gradient):
        return sharded(functools.partial(body_square, momentum.shape[1]))(momentum, gradient)

    if (row_devices, column_devices) != (ROW_DEVICES, COLUMN_DEVICES):
        return general
    return square
```

```python
import functools
import math

import jax
import jax.numpy as jnp
from jax import lax
from jax.experimental import pallas as pl
from jax.experimental.pallas import tpu as pltpu
from jax.sharding import PartitionSpec as P


STEPS = 2


momentum_decay = 0.95
linear_term = 3.4445
cubic_term = -4.775
quintic_term = 2.0315

f32, bf16 = jnp.float32, jnp.bfloat16


def dot_nn(a, b):
    return lax.dot_general(a, b, (((1,), (0,)), ((), ())), preferred_element_type=f32)


def dot_nt(a, b):
    return lax.dot_general(a, b, (((1,), (1,)), ((), ())), preferred_element_type=f32)


def iterate_general(current):
    matrix = current.astype(bf16)
    column_panel = lax.all_gather(matrix, "dp", axis=0, tiled=True)
    summed_part = lax.psum_scatter(dot_nt(matrix, column_panel), "shard", scatter_dimension=0, tiled=True)
    gram_part = summed_part.astype(bf16)
    gram_panel = lax.all_gather(gram_part, "shard", axis=0, tiled=True)
    square_sum = lax.psum(jnp.sum(jnp.square(gram_part.astype(f32))), ("dp", "shard"))
    inverse_norm = lax.rsqrt(square_sum)
    root_scale = jnp.sqrt(inverse_norm)
    matrix_full = matrix.astype(f32)
    first = dot_nn(gram_panel, column_panel)
    mixture = (
        cubic_term * root_scale * matrix_full + quintic_term * root_scale * inverse_norm * first
    ).astype(bf16)
    second = dot_nn(gram_panel, lax.all_gather(mixture, "dp", axis=0, tiled=True))
    return linear_term * root_scale * matrix_full + inverse_norm * second


def x_bit(i):
    return (i >> 1) & 1


def y_bit(i):
    return (i >> 2) & 1


def x_pick(i):
    return i ^ 2 ^ x_bit(i)


def y_pick(i):
    return i ^ 4 ^ (x_bit(i) ^ y_bit(i))


ROW_DEVICES = 8
COLUMN_DEVICES = 4
VMEM_LIMIT = 16 << 20
CORE = [(i, i ^ 1) for i in range(ROW_DEVICES)]
TAKE_X = [(x_pick(i), i) for i in range(ROW_DEVICES)]
TAKE_Y = [(y_pick(i), i) for i in range(ROW_DEVICES)]
GIVE_X = [(i, x_pick(i)) for i in range(ROW_DEVICES)]
GIVE_Y = [(i, y_pick(i)) for i in range(ROW_DEVICES)]


def over_dp(value, pairs):
    return lax.ppermute(value, "dp", pairs)


def call(kernel, outs, args, scalars=(), scratch=(), flops=0, streamed=False):
    moved = sum(a.size * a.dtype.itemsize for a in [*args, *outs])
    vmem = pl.BlockSpec(memory_space=pltpu.VMEM)
    return pl.pallas_call(
        kernel,
        out_shape=outs,
        in_specs=[pl.BlockSpec(memory_space=pltpu.SMEM)] * len(scalars) + [vmem] * len(args),
        out_specs=[pl.BlockSpec(memory_space=pl.ANY) if streamed else vmem] * len(outs),
        scratch_shapes=list(scratch),
        compiler_params=pltpu.CompilerParams(vmem_limit_bytes=VMEM_LIMIT),
        cost_estimate=pl.CostEstimate(flops=flops, bytes_accessed=moved, transcendentals=0),
    )(*scalars, *[pltpu.with_memory_space_constraint(a, pltpu.VMEM) for a in args])


def rows_at(z, k, rows):
    return pl.ds(pl.multiple_of((z ^ k) * rows, rows), rows)


def split_rows(total, z, outs):
    rows = outs[0].shape[1]
    for k, out in enumerate(outs):
        out[...] = total[:, rows_at(z, k, rows), :].astype(out.dtype)


def own_gram_kernel(z_ref, core_ref, top, bottom, core_top, core_bottom, *rest):
    outs, total = rest[:-1], rest[-1]
    for q, (left, right) in enumerate([(top, top), (bottom, bottom), (bottom, top)]):
        total[q] = dot_nt(left[...], right[...])
    for core, (first, second) in enumerate([(core_top, core_bottom), (core_bottom, core_top)]):

        @pl.when(core_ref[0] == core)
        def _():
            total[3] = dot_nt(top[...], first[...])
            total[4] = dot_nt(bottom[...], second[...])

    split_rows(total, z_ref[0], outs)


def stacked(top, bottom):
    return jnp.concatenate([top[...], bottom[...]], axis=0)


def early_gram_kernel(z_ref, top, bottom, x_bottom, y_top, *rest):
    outs, total = rest[:-1], rest[-1]
    half = top.shape[0]
    own = stacked(top, bottom)
    for q, right in ((0, x_bottom), (3, y_top)):
        value = dot_nt(own, right[...])
        total[q], total[q + 1] = value[:half], value[half:]
    total[2] = dot_nt(x_bottom[...], y_top[...])
    split_rows(total, z_ref[0], outs)


def late_gram_kernel(z_ref, top, bottom, x_top, x_bottom, y_top, y_bottom, *rest):
    outs, total = rest[:-1], rest[-1]
    half = top.shape[0]
    own = stacked(top, bottom)
    for q, right in ((0, x_top), (5, y_bottom)):
        value = dot_nt(own, right[...])
        total[q], total[q + 1] = value[:half], value[half:]
    total[2] = dot_nt(x_top[...], y_top[...])
    value = dot_nt(stacked(x_top, x_bottom), y_bottom[...])
    total[3], total[4] = value[:half], value[half:]
    split_rows(total, z_ref[0], outs)


def gram(kernel, shape, scalars, halves):
    count, rows, columns = shape
    shape = (count, rows // COLUMN_DEVICES, columns)
    return call(
        kernel,
        [jax.ShapeDtypeStruct(shape, kind) for kind in (f32, bf16, f32, bf16)],
        halves,
        scalars,
        [pltpu.VMEM((count, rows, columns), f32)],
        2 * count * rows * columns * halves[0].shape[1],
    )


def own_assemble_kernel(z_ref, *refs):
    parts, (diagonal, beside) = refs[:-2], refs[-2:]
    rows, half = parts[0].shape[1:]
    for k, part in enumerate(parts):
        at = rows_at(z_ref[0], k, rows)
        lower = pl.ds(pl.multiple_of(half + at.start, rows), rows)
        diagonal[at, :half] = part[0]
        diagonal[lower, half:] = part[1]
        diagonal[lower, :half] = part[2]
        beside[at, :] = part[3]
        beside[lower, :] = part[4]
    diagonal[:half, half:] = diagonal[half:, :half].T


def own_assemble(z, parts):
    half = parts[0].shape[2]
    outs = [jax.ShapeDtypeStruct((2 * half, columns), bf16) for columns in (2 * half, half)]
    return call(own_assemble_kernel, outs, parts, [z])


def beside_kernel(core_ref, own, other, out):
    half = own.shape[1]
    for core in range(2):

        @pl.when(core_ref[0] == core)
        def _():
            like, unlike = slice(core * half, (core + 1) * half), slice((1 - core) * half, (2 - core) * half)
            out[:half, like] = own[:half]
            out[half:, unlike] = own[half:]
            out[unlike, :half] = other[:half].T
            out[like, half:] = other[half:].T


def beside_of(core, own, other):
    rows = own.shape[0]
    return call(beside_kernel, [jax.ShapeDtypeStruct((rows, rows), bf16)], [own, other], [core])[0]


def near_assemble_kernel(z_ref, *refs):
    parts, near, wholes = refs[:COLUMN_DEVICES], refs[COLUMN_DEVICES], refs[COLUMN_DEVICES + 1 :]
    count, rows, half = parts[0].shape
    for k, part in enumerate(parts):
        at = rows_at(z_ref[0], k, rows)
        lower = pl.ds(pl.multiple_of(half + at.start, rows), rows)
        near[at, :half] = part[0]
        near[lower, :half] = part[1]
        near[at, half:] = part[count - 2]
        near[lower, half:] = part[count - 1]
        for w, whole in enumerate(wholes):
            whole[:, at, :] = part[2 * w : count - 2 + 2 * w]


def near_assemble(z, parts, with_wholes):
    count, _, half = parts[0].shape
    outs = [jax.ShapeDtypeStruct((2 * half, 2 * half), bf16)]
    if with_wholes:
        outs += [jax.ShapeDtypeStruct((count - 2, half, half), bf16)] * 2
    return call(near_assemble_kernel, outs, parts, [z])


def mirror_assemble_kernel(z_ref, *refs):
    x_early, y_early, *late, side, linked, crossed, x_late, y_late = refs
    rows, half = late[0].shape[1:]
    for shifts, x_part, y_part in zip(((0,), (1, 2), (3,)), late[::2], late[1::2]):
        for k, shift in enumerate(shifts):
            at = rows_at(z_ref[0], shift, rows)
            x_late[:, at, :] = x_part[:, k * rows : (k + 1) * rows]
            y_late[:, at, :] = y_part[:, k * rows : (k + 1) * rows]
    columns = [slice(k * half, (k + 1) * half) for k in range(4)]
    top, bottom = columns[0], columns[1]
    for k in range(2):
        side[top, columns[k]] = x_late[k].T
        side[bottom, columns[k]] = x_early[k].T
        side[top, columns[2 + k]] = y_early[1 + k].T
        side[bottom, columns[2 + k]] = y_late[3 + k].T
    linked[top, top] = x_late[2]
    linked[bottom, top] = x_early[2]
    linked[top, bottom] = y_early[0].T
    linked[bottom, bottom] = y_late[2].T
    crossed[top, top] = x_late[3]
    crossed[bottom, top] = x_late[4]
    crossed[top, bottom] = y_late[0].T
    crossed[bottom, bottom] = y_late[1].T


def mirror_assemble(z, mirrored):
    count, _, half = mirrored[-1].shape
    outs = [jax.ShapeDtypeStruct((2 * half, width * half), bf16) for width in (4, 2, 2)]
    return call(mirror_assemble_kernel, outs, mirrored, [z], [pltpu.VMEM((count, half, half), bf16)] * 2)


def product_kernel(n_grams, n_halves, has_sum, finish, tile, stream, *refs):
    refs = list(refs)
    if stream:
        streamed, held, arrived = refs[-3:]
        refs = refs[:-3] + [held]

        def column_copy(t):
            at = pl.ds(pl.multiple_of(t * tile, tile), tile)
            return pltpu.make_async_copy(held.at[:, at], streamed.at[:, at], arrived.at[t])

    if finish:
        inverse_norm = lax.rsqrt(jnp.sum(refs.pop(0)[...], axis=(0, 1), keepdims=True))
        root_scale = jnp.sqrt(inverse_norm)
        scales = finish(root_scale, inverse_norm)
    grams, refs = refs[:n_grams], refs[n_grams:]
    halves, refs = refs[:n_halves], refs[n_halves:]
    summed = refs.pop(0) if has_sum else None
    own, outs = (refs[:2], refs[2:]) if finish else (None, refs)
    columns = halves[0].shape[1]

    def column_tile(t, carry):
        at = pl.ds(pl.multiple_of(t * tile, tile), tile)
        gram = jnp.concatenate([g[...] for g in grams], axis=1)
        value = dot_nn(gram, jnp.concatenate([h[:, at] for h in halves], axis=0))
        if has_sum:
            value = value + summed[:, at]
        if finish:
            block = jnp.concatenate([own[0][:, at], own[1][:, at]], axis=0)
            value = scales[0] * block.astype(f32) + scales[1] * value
        rows = value.shape[0] // len(outs)
        for k, out in enumerate(outs):
            out[:, at] = value[k * rows : (k + 1) * rows].astype(out.dtype)
        if stream:
            column_copy(t).start()
        return carry

    lax.fori_loop(0, columns // tile, column_tile, 0)
    if stream:

        def wait(t, carry):
            column_copy(t).wait()
            return carry

        lax.fori_loop(0, columns // tile, wait, 0)


def product(grams, halves, summed=None, finish=None, dtype=f32, parts=1):
    half, columns = halves[0].shape
    tile = 256 if columns % 256 == 0 else columns
    args = ([finish[1]] if finish else []) + list(grams) + list(halves)
    args += [] if summed is None else [summed]
    args += list(finish[2]) if finish else []
    outs = [jax.ShapeDtypeStruct((2 * half // parts, columns), dtype)] * parts
    stream = bool(finish) and parts == 1
    return call(
        functools.partial(
            product_kernel, len(grams), len(halves), summed is not None, finish and finish[0], tile, stream
        ),
        outs,
        args,
        scratch=[pltpu.VMEM(outs[0].shape, dtype), pltpu.SemaphoreType.DMA((columns // tile,))] if stream else (),
        streamed=stream,
        flops=4 * half * half * columns * len(halves),
    )


def exchanged(value, distance):
    return lax.ppermute(value, "shard", [(z, z ^ distance) for z in range(COLUMN_DEVICES)])


def total_of(value):
    value = value + over_dp(value, CORE)
    x_side, y_side, diagonal = (over_dp(value, [(i, i ^ k) for i in range(ROW_DEVICES)]) for k in (2, 4, 6))
    return (value + x_side) + (y_side + diagonal)


def gather(block):
    top, bottom = block
    x_bottom, y_top = over_dp(bottom, TAKE_X), over_dp(top, TAKE_Y)
    x_top, y_bottom = over_dp(top, TAKE_X), over_dp(bottom, TAKE_Y)
    core = over_dp(top, CORE), over_dp(bottom, CORE)
    d_oth_bottom, d_sel_top = over_dp(x_bottom, GIVE_Y), over_dp(y_top, GIVE_X)
    x_oth_bottom, y_oth_top = over_dp(x_bottom, CORE), over_dp(y_top, CORE)
    x_oth_top, y_oth_bottom = over_dp(x_top, CORE), over_dp(y_bottom, CORE)
    side = x_oth_top, x_oth_bottom, y_oth_top, y_oth_bottom
    crossed = over_dp(d_oth_bottom, CORE), over_dp(d_sel_top, CORE)
    return core, (x_bottom, y_top), (x_top, y_bottom), side, (d_sel_top, d_oth_bottom), crossed


def add_kernel(kept, *refs):
    total = kept[...]
    for piece in refs[:-1]:
        total = total + piece[...].astype(f32)
    refs[-1][...] = total.astype(bf16)


def reduce_parts(pieces):
    kept, one, passed, three = pieces
    three, one = exchanged(three, 1), exchanged(one, 1)
    out = jax.ShapeDtypeStruct(kept.shape, bf16)
    (two,) = call(add_kernel, [out], [passed, three])
    two = exchanged(two, 2)
    return call(add_kernel, [out], [kept, one, two])[0]


def squares_kernel(weights, *refs):
    *parts, before, out = refs
    total = before[...]
    for part, part_weights in zip(parts, weights):
        for weight in sorted(set(part_weights)):
            square = sum(jnp.square(part[q].astype(f32)) for q, w in enumerate(part_weights) if w == weight)
            square = sum(square[:, k : k + 128] for k in range(0, square.shape[1], 128))
            total = total + weight * jnp.sum(square.reshape(-1, 8, 128), axis=0)
    out[...] = total


def squares_of(parts, weights, before):
    out = jax.ShapeDtypeStruct(before.shape, f32)
    return call(functools.partial(squares_kernel, weights), [out], [*parts, before])[0]


def spread(part):
    two, one = exchanged(part, 2), exchanged(part, 1)
    three = exchanged(two, 1)
    return [part, one, two, three]


def iterate_square(matrix, gain, dtype, parts):
    z = lax.axis_index("shard").reshape(1)
    side_index = (lax.axis_index("dp") & 1).reshape(1)
    core, one, two, side, linked, crossed = gather(matrix)
    (x_bottom, y_top), (x_top, y_bottom) = one, two
    half = matrix[0].shape[0]
    own_pieces = gram(own_gram_kernel, (5, half, half), [z, side_index], [*matrix, *core])
    own_part = reduce_parts(own_pieces)
    own_parts = spread(own_part)
    early_pieces = gram(early_gram_kernel, (5, half, half), [z], [*matrix, x_bottom, y_top])
    early_part = reduce_parts(early_pieces)
    late_pieces = gram(
        late_gram_kernel, (7, half, half), [z], [*matrix, x_top, x_bottom, y_top, y_bottom]
    )
    late_part = reduce_parts(late_pieces)
    early_parts = spread(early_part)
    late_parts = spread(late_part)
    zeros = jnp.zeros((8, 128), f32)
    last_squares = exchanged(squares_of([late_part], [(2.0,) * 7], zeros), 3)
    weights = [(1.0, 1.0, 2.0, 2.0, 2.0)] * 4 + [(2.0,) * 5] * 4 + [(2.0,) * 7] * 3
    squares = squares_of([*own_parts, *early_parts, *late_parts[:3]], weights, last_squares)
    squares = total_of(squares)
    near_one, x_whole, y_whole = near_assemble(z, early_parts, True)
    early = over_dp(x_whole, GIVE_X), over_dp(y_whole, GIVE_Y)
    late = []
    for shifts in ((0,), (1, 2), (3,)):
        x_part, y_part = late_parts[shifts[0]][:-2], late_parts[shifts[0]][2:]
        if len(shifts) > 1:
            x_part = jnp.concatenate([late_parts[k][:-2] for k in shifts], axis=1)
            y_part = jnp.concatenate([late_parts[k][2:] for k in shifts], axis=1)
        late += [over_dp(x_part, GIVE_X), over_dp(y_part, GIVE_Y)]
    own, beside = own_assemble(z, own_parts)
    beside = beside_of(side_index, beside, over_dp(beside, CORE))
    (near_two,) = near_assemble(z, late_parts, False)
    side_gram, linked_gram, crossed_gram = mirror_assemble(z, [*early, *late])

    def mixing(root_scale, inverse_norm):
        return cubic_term * root_scale, quintic_term * root_scale * inverse_norm

    def ending(root_scale, inverse_norm):
        return gain * linear_term * root_scale, gain * inverse_norm

    (first,) = product([own, beside], [*matrix, *core])
    (first,) = product([near_one, near_two], [*one, *two], first)
    mixture = product(
        [side_gram, linked_gram, crossed_gram],
        [*side, *linked, *crossed],
        first,
        (mixing, squares, matrix),
        bf16,
        2,
    )
    core, one, two, side, linked, crossed = gather(mixture)
    (second,) = product([own, beside], [*mixture, *core])
    (second,) = product([near_one], one, second)
    (second,) = product([near_two, side_gram], [*two, *side], second)
    (second,) = product([linked_gram], linked, second)
    return product([crossed_gram], crossed, second, (ending, squares, matrix), dtype, parts)


def current_of(momentum, gradient):
    grad_full = gradient.astype(f32)
    new_momentum = momentum_decay * momentum + grad_full
    return new_momentum, grad_full + momentum_decay * new_momentum


def body_square(columns, momentum, gradient):
    half = momentum.shape[0] // 2
    block = [
        current_of(momentum[rows], gradient[rows])[1].astype(bf16)
        for rows in (slice(0, half), slice(half, None))
    ]
    new_momentum, _ = current_of(*lax.optimization_barrier((momentum, gradient)))
    for iteration in range(STEPS):
        last = iteration == STEPS - 1
        block = iterate_square(
            block, math.sqrt(columns) if last else 1.0, f32 if last else bf16, 1 if last else 2
        )
    return (new_momentum, block[0])


def body_general(columns, momentum, gradient):
    grad_full = gradient.astype(f32)
    new_momentum = momentum_decay * momentum + grad_full
    current = grad_full + momentum_decay * new_momentum
    for _ in range(STEPS):
        current = iterate_general(current)
    return (new_momentum, math.sqrt(columns) * current)


def solution(mesh):
    row_devices, column_devices = mesh.shape["dp"], mesh.shape["shard"]
    spec = P("dp", "shard")

    def sharded(body):
        return jax.shard_map(body, mesh=mesh, in_specs=(spec, spec), out_specs=(spec, spec), check_vma=False)

    def general(momentum, gradient):
        return sharded(functools.partial(body_general, momentum.shape[1]))(momentum, gradient)

    def square(momentum, gradient):
        return sharded(functools.partial(body_square, momentum.shape[1]))(momentum, gradient)

    if (row_devices, column_devices) != (ROW_DEVICES, COLUMN_DEVICES):
        return general
    return square
```

```python
import functools
import math

import jax
import jax.numpy as jnp
from jax import lax
from jax.experimental import pallas as pl
from jax.experimental.pallas import tpu as pltpu
from jax.sharding import PartitionSpec as P


STEPS = 2


momentum_decay = 0.95
linear_term = 3.4445
cubic_term = -4.775
quintic_term = 2.0315

f32, bf16 = jnp.float32, jnp.bfloat16


def dot_nn(a, b):
    return lax.dot_general(a, b, (((1,), (0,)), ((), ())), preferred_element_type=f32)


def dot_nt(a, b):
    return lax.dot_general(a, b, (((1,), (1,)), ((), ())), preferred_element_type=f32)


def iterate_general(current):
    matrix = current.astype(bf16)
    column_panel = lax.all_gather(matrix, "dp", axis=0, tiled=True)
    summed_part = lax.psum_scatter(dot_nt(matrix, column_panel), "shard", scatter_dimension=0, tiled=True)
    gram_part = summed_part.astype(bf16)
    gram_panel = lax.all_gather(gram_part, "shard", axis=0, tiled=True)
    square_sum = lax.psum(jnp.sum(jnp.square(gram_part.astype(f32))), ("dp", "shard"))
    inverse_norm = lax.rsqrt(square_sum)
    root_scale = jnp.sqrt(inverse_norm)
    matrix_full = matrix.astype(f32)
    first = dot_nn(gram_panel, column_panel)
    mixture = (
        cubic_term * root_scale * matrix_full + quintic_term * root_scale * inverse_norm * first
    ).astype(bf16)
    second = dot_nn(gram_panel, lax.all_gather(mixture, "dp", axis=0, tiled=True))
    return linear_term * root_scale * matrix_full + inverse_norm * second


def x_bit(i):
    return (i >> 1) & 1


def y_bit(i):
    return (i >> 2) & 1


def x_pick(i):
    return i ^ 2 ^ x_bit(i)


def y_pick(i):
    return i ^ 4 ^ (x_bit(i) ^ y_bit(i))


ROW_DEVICES = 8
COLUMN_DEVICES = 4
VMEM_LIMIT = 16 << 20
CORE = [(i, i ^ 1) for i in range(ROW_DEVICES)]
TAKE_X = [(x_pick(i), i) for i in range(ROW_DEVICES)]
TAKE_Y = [(y_pick(i), i) for i in range(ROW_DEVICES)]
GIVE_X = [(i, x_pick(i)) for i in range(ROW_DEVICES)]
GIVE_Y = [(i, y_pick(i)) for i in range(ROW_DEVICES)]


def over_dp(value, pairs):
    return lax.ppermute(value, "dp", pairs)


def call(kernel, outs, args, scalars=(), scratch=(), flops=0, streamed=False):
    moved = sum(a.size * a.dtype.itemsize for a in [*args, *outs])
    vmem = pl.BlockSpec(memory_space=pltpu.VMEM)
    return pl.pallas_call(
        kernel,
        out_shape=outs,
        in_specs=[pl.BlockSpec(memory_space=pltpu.SMEM)] * len(scalars) + [vmem] * len(args),
        out_specs=[pl.BlockSpec(memory_space=pl.ANY) if streamed else vmem] * len(outs),
        scratch_shapes=list(scratch),
        compiler_params=pltpu.CompilerParams(vmem_limit_bytes=VMEM_LIMIT),
        cost_estimate=pl.CostEstimate(flops=flops, bytes_accessed=moved, transcendentals=0),
    )(*scalars, *[pltpu.with_memory_space_constraint(a, pltpu.VMEM) for a in args])


def rows_at(z, k, rows):
    return pl.ds(pl.multiple_of((z ^ k) * rows, rows), rows)


def split_rows(total, z, outs):
    rows = outs[0].shape[1]
    for k, out in enumerate(outs):
        out[...] = total[:, rows_at(z, k, rows), :].astype(out.dtype)


def own_gram_kernel(z_ref, core_ref, top, bottom, core_top, core_bottom, *rest):
    outs, total = rest[:-1], rest[-1]
    for q, (left, right) in enumerate([(top, top), (bottom, bottom), (bottom, top)]):
        total[q] = dot_nt(left[...], right[...])
    for core, (first, second) in enumerate([(core_top, core_bottom), (core_bottom, core_top)]):

        @pl.when(core_ref[0] == core)
        def _():
            total[3] = dot_nt(top[...], first[...])
            total[4] = dot_nt(bottom[...], second[...])

    split_rows(total, z_ref[0], outs)


def stacked(top, bottom):
    return jnp.concatenate([top[...], bottom[...]], axis=0)


def early_gram_kernel(z_ref, top, bottom, x_bottom, y_top, *rest):
    outs, total = rest[:-1], rest[-1]
    half = top.shape[0]
    own = stacked(top, bottom)
    for q, right in ((0, x_bottom), (3, y_top)):
        value = dot_nt(own, right[...])
        total[q], total[q + 1] = value[:half], value[half:]
    total[2] = dot_nt(x_bottom[...], y_top[...])
    split_rows(total, z_ref[0], outs)


def late_gram_kernel(z_ref, top, bottom, x_top, x_bottom, y_top, y_bottom, *rest):
    outs, total = rest[:-1], rest[-1]
    half = top.shape[0]
    own = stacked(top, bottom)
    for q, right in ((0, x_top), (5, y_bottom)):
        value = dot_nt(own, right[...])
        total[q], total[q + 1] = value[:half], value[half:]
    total[2] = dot_nt(x_top[...], y_top[...])
    value = dot_nt(stacked(x_top, x_bottom), y_bottom[...])
    total[3], total[4] = value[:half], value[half:]
    split_rows(total, z_ref[0], outs)


def gram(kernel, shape, scalars, halves):
    count, rows, columns = shape
    shape = (count, rows // COLUMN_DEVICES, columns)
    return call(
        kernel,
        [jax.ShapeDtypeStruct(shape, kind) for kind in (f32, bf16, f32, bf16)],
        halves,
        scalars,
        [pltpu.VMEM((count, rows, columns), f32)],
        2 * count * rows * columns * halves[0].shape[1],
    )


def own_assemble_kernel(z_ref, *refs):
    parts, (diagonal, beside) = refs[:-2], refs[-2:]
    rows, half = parts[0].shape[1:]
    for k, part in enumerate(parts):
        at = rows_at(z_ref[0], k, rows)
        lower = pl.ds(pl.multiple_of(half + at.start, rows), rows)
        diagonal[at, :half] = part[0]
        diagonal[lower, half:] = part[1]
        diagonal[lower, :half] = part[2]
        beside[at, :] = part[3]
        beside[lower, :] = part[4]
    diagonal[:half, half:] = diagonal[half:, :half].T


def own_assemble(z, parts):
    half = parts[0].shape[2]
    outs = [jax.ShapeDtypeStruct((2 * half, columns), bf16) for columns in (2 * half, half)]
    return call(own_assemble_kernel, outs, parts, [z])


def beside_kernel(core_ref, own, other, out):
    half = own.shape[1]
    for core in range(2):

        @pl.when(core_ref[0] == core)
        def _():
            like, unlike = slice(core * half, (core + 1) * half), slice((1 - core) * half, (2 - core) * half)
            out[:half, like] = own[:half]
            out[half:, unlike] = own[half:]
            out[unlike, :half] = other[:half].T
            out[like, half:] = other[half:].T


def beside_of(core, own, other):
    rows = own.shape[0]
    return call(beside_kernel, [jax.ShapeDtypeStruct((rows, rows), bf16)], [own, other], [core])[0]


def near_assemble_kernel(z_ref, *refs):
    parts, near, wholes = refs[:COLUMN_DEVICES], refs[COLUMN_DEVICES], refs[COLUMN_DEVICES + 1 :]
    count, rows, half = parts[0].shape
    for k, part in enumerate(parts):
        at = rows_at(z_ref[0], k, rows)
        lower = pl.ds(pl.multiple_of(half + at.start, rows), rows)
        near[at, :half] = part[0]
        near[lower, :half] = part[1]
        near[at, half:] = part[count - 2]
        near[lower, half:] = part[count - 1]
        for w, whole in enumerate(wholes):
            whole[:, at, :] = part[2 * w : count - 2 + 2 * w]


def near_assemble(z, parts, with_wholes):
    count, _, half = parts[0].shape
    outs = [jax.ShapeDtypeStruct((2 * half, 2 * half), bf16)]
    if with_wholes:
        outs += [jax.ShapeDtypeStruct((count - 2, half, half), bf16)] * 2
    return call(near_assemble_kernel, outs, parts, [z])


def mirror_assemble_kernel(z_ref, *refs):
    x_early, y_early, *late, side, linked, crossed, x_late, y_late = refs
    rows, half = late[0].shape[1:]
    for shifts, x_part, y_part in zip(((0,), (1, 2), (3,)), late[::2], late[1::2]):
        for k, shift in enumerate(shifts):
            at = rows_at(z_ref[0], shift, rows)
            x_late[:, at, :] = x_part[:, k * rows : (k + 1) * rows]
            y_late[:, at, :] = y_part[:, k * rows : (k + 1) * rows]
    columns = [slice(k * half, (k + 1) * half) for k in range(4)]
    top, bottom = columns[0], columns[1]
    for k in range(2):
        side[top, columns[k]] = x_late[k].T
        side[bottom, columns[k]] = x_early[k].T
        side[top, columns[2 + k]] = y_early[1 + k].T
        side[bottom, columns[2 + k]] = y_late[3 + k].T
    linked[top, top] = x_late[2]
    linked[bottom, top] = x_early[2]
    linked[top, bottom] = y_early[0].T
    linked[bottom, bottom] = y_late[2].T
    crossed[top, top] = x_late[3]
    crossed[bottom, top] = x_late[4]
    crossed[top, bottom] = y_late[0].T
    crossed[bottom, bottom] = y_late[1].T


def mirror_assemble(z, mirrored):
    count, _, half = mirrored[-1].shape
    outs = [jax.ShapeDtypeStruct((2 * half, width * half), bf16) for width in (4, 2, 2)]
    return call(mirror_assemble_kernel, outs, mirrored, [z], [pltpu.VMEM((count, half, half), bf16)] * 2)


def product_kernel(n_grams, n_halves, has_sum, finish, tile, stream, *refs):
    refs = list(refs)
    if stream:
        streamed, held, arrived = refs[-3:]
        refs = refs[:-3] + [held]

        def column_copy(t):
            at = pl.ds(pl.multiple_of(t * tile, tile), tile)
            return pltpu.make_async_copy(held.at[:, at], streamed.at[:, at], arrived.at[t])

    if finish:
        inverse_norm = lax.rsqrt(jnp.sum(refs.pop(0)[...], axis=(0, 1), keepdims=True))
        root_scale = jnp.sqrt(inverse_norm)
        scales = finish(root_scale, inverse_norm)
    grams, refs = refs[:n_grams], refs[n_grams:]
    halves, refs = refs[:n_halves], refs[n_halves:]
    summed = refs.pop(0) if has_sum else None
    own, outs = (refs[:2], refs[2:]) if finish else (None, refs)
    columns = halves[0].shape[1]

    def column_tile(t, carry):
        at = pl.ds(pl.multiple_of(t * tile, tile), tile)
        gram = jnp.concatenate([g[...] for g in grams], axis=1)
        value = dot_nn(gram, jnp.concatenate([h[:, at] for h in halves], axis=0))
        if has_sum:
            value = value + summed[:, at]
        if finish:
            block = jnp.concatenate([own[0][:, at], own[1][:, at]], axis=0)
            value = scales[0] * block.astype(f32) + scales[1] * value
        rows = value.shape[0] // len(outs)
        for k, out in enumerate(outs):
            out[:, at] = value[k * rows : (k + 1) * rows].astype(out.dtype)
        if stream:
            column_copy(t).start()
        return carry

    lax.fori_loop(0, columns // tile, column_tile, 0)
    if stream:

        def wait(t, carry):
            column_copy(t).wait()
            return carry

        lax.fori_loop(0, columns // tile, wait, 0)


def product(grams, halves, summed=None, finish=None, dtype=f32, parts=1, wide=False):
    half, columns = halves[0].shape
    tile = columns if wide or columns % 256 else 256
    args = ([finish[1]] if finish else []) + list(grams) + list(halves)
    args += [] if summed is None else [summed]
    args += list(finish[2]) if finish else []
    outs = [jax.ShapeDtypeStruct((2 * half // parts, columns), dtype)] * parts
    stream = bool(finish) and parts == 1
    return call(
        functools.partial(
            product_kernel, len(grams), len(halves), summed is not None, finish and finish[0], tile, stream
        ),
        outs,
        args,
        scratch=[pltpu.VMEM(outs[0].shape, dtype), pltpu.SemaphoreType.DMA((columns // tile,))] if stream else (),
        streamed=stream,
        flops=4 * half * half * columns * len(halves),
    )


def exchanged(value, distance):
    return lax.ppermute(value, "shard", [(z, z ^ distance) for z in range(COLUMN_DEVICES)])


def total_of(value):
    value = value + over_dp(value, CORE)
    x_side, y_side, diagonal = (over_dp(value, [(i, i ^ k) for i in range(ROW_DEVICES)]) for k in (2, 4, 6))
    return (value + x_side) + (y_side + diagonal)


def gather(block):
    top, bottom = block
    x_bottom, y_top = over_dp(bottom, TAKE_X), over_dp(top, TAKE_Y)
    x_top, y_bottom = over_dp(top, TAKE_X), over_dp(bottom, TAKE_Y)
    core = over_dp(top, CORE), over_dp(bottom, CORE)
    d_oth_bottom, d_sel_top = over_dp(x_bottom, GIVE_Y), over_dp(y_top, GIVE_X)
    x_oth_bottom, y_oth_top = over_dp(x_bottom, CORE), over_dp(y_top, CORE)
    x_oth_top, y_oth_bottom = over_dp(x_top, CORE), over_dp(y_bottom, CORE)
    side = x_oth_top, x_oth_bottom, y_oth_top, y_oth_bottom
    crossed = over_dp(d_oth_bottom, CORE), over_dp(d_sel_top, CORE)
    return core, (x_bottom, y_top), (x_top, y_bottom), side, (d_sel_top, d_oth_bottom), crossed


def add_kernel(kept, *refs):
    total = kept[...]
    for piece in refs[:-1]:
        total = total + piece[...].astype(f32)
    refs[-1][...] = total.astype(bf16)


def reduce_parts(pieces):
    kept, one, passed, three = pieces
    three, one = exchanged(three, 1), exchanged(one, 1)
    out = jax.ShapeDtypeStruct(kept.shape, bf16)
    (two,) = call(add_kernel, [out], [passed, three])
    two = exchanged(two, 2)
    return call(add_kernel, [out], [kept, one, two])[0]


def squares_kernel(weights, *refs):
    *parts, before, out = refs
    total = before[...]
    for part, part_weights in zip(parts, weights):
        for weight in sorted(set(part_weights)):
            square = sum(jnp.square(part[q].astype(f32)) for q, w in enumerate(part_weights) if w == weight)
            square = sum(square[:, k : k + 128] for k in range(0, square.shape[1], 128))
            total = total + weight * jnp.sum(square.reshape(-1, 8, 128), axis=0)
    out[...] = total


def squares_of(parts, weights, before):
    out = jax.ShapeDtypeStruct(before.shape, f32)
    return call(functools.partial(squares_kernel, weights), [out], [*parts, before])[0]


def spread(part):
    two, one = exchanged(part, 2), exchanged(part, 1)
    three = exchanged(two, 1)
    return [part, one, two, three]


def iterate_square(matrix, gain, dtype, parts):
    z = lax.axis_index("shard").reshape(1)
    side_index = (lax.axis_index("dp") & 1).reshape(1)
    core, one, two, side, linked, crossed = gather(matrix)
    (x_bottom, y_top), (x_top, y_bottom) = one, two
    half = matrix[0].shape[0]
    own_pieces = gram(own_gram_kernel, (5, half, half), [z, side_index], [*matrix, *core])
    own_part = reduce_parts(own_pieces)
    own_parts = spread(own_part)
    early_pieces = gram(early_gram_kernel, (5, half, half), [z], [*matrix, x_bottom, y_top])
    early_part = reduce_parts(early_pieces)
    late_pieces = gram(
        late_gram_kernel, (7, half, half), [z], [*matrix, x_top, x_bottom, y_top, y_bottom]
    )
    late_part = reduce_parts(late_pieces)
    early_parts = spread(early_part)
    late_parts = spread(late_part)
    zeros = jnp.zeros((8, 128), f32)
    last_squares = exchanged(squares_of([late_part], [(2.0,) * 7], zeros), 3)
    weights = [(1.0, 1.0, 2.0, 2.0, 2.0)] * 4 + [(2.0,) * 5] * 4 + [(2.0,) * 7] * 3
    squares = squares_of([*own_parts, *early_parts, *late_parts[:3]], weights, last_squares)
    squares = total_of(squares)
    near_one, x_whole, y_whole = near_assemble(z, early_parts, True)
    early = over_dp(x_whole, GIVE_X), over_dp(y_whole, GIVE_Y)
    late = []
    for shifts in ((0,), (1, 2), (3,)):
        x_part, y_part = late_parts[shifts[0]][:-2], late_parts[shifts[0]][2:]
        if len(shifts) > 1:
            x_part = jnp.concatenate([late_parts[k][:-2] for k in shifts], axis=1)
            y_part = jnp.concatenate([late_parts[k][2:] for k in shifts], axis=1)
        late += [over_dp(x_part, GIVE_X), over_dp(y_part, GIVE_Y)]
    own, beside = own_assemble(z, own_parts)
    beside = beside_of(side_index, beside, over_dp(beside, CORE))
    (near_two,) = near_assemble(z, late_parts, False)
    side_gram, linked_gram, crossed_gram = mirror_assemble(z, [*early, *late])

    def mixing(root_scale, inverse_norm):
        return cubic_term * root_scale, quintic_term * root_scale * inverse_norm

    def ending(root_scale, inverse_norm):
        return gain * linear_term * root_scale, gain * inverse_norm

    (first,) = product([own, beside], [*matrix, *core])
    (first,) = product([near_one, near_two], [*one, *two], first)
    mixture = product(
        [side_gram, linked_gram, crossed_gram],
        [*side, *linked, *crossed],
        first,
        (mixing, squares, matrix),
        bf16,
        2,
        True,
    )
    core, one, two, side, linked, crossed = gather(mixture)
    (second,) = product([own, beside], [*mixture, *core])
    (second,) = product([near_one], one, second)
    (second,) = product([near_two, side_gram], [*two, *side], second)
    (second,) = product([linked_gram], linked, second, wide=True)
    return product([crossed_gram], crossed, second, (ending, squares, matrix), dtype, parts, parts == 2)


def current_of(momentum, gradient):
    grad_full = gradient.astype(f32)
    new_momentum = momentum_decay * momentum + grad_full
    return new_momentum, grad_full + momentum_decay * new_momentum


def body_square(columns, momentum, gradient):
    half = momentum.shape[0] // 2
    block = [
        current_of(momentum[rows], gradient[rows])[1].astype(bf16)
        for rows in (slice(0, half), slice(half, None))
    ]
    new_momentum, _ = current_of(*lax.optimization_barrier((momentum, gradient)))
    for iteration in range(STEPS):
        last = iteration == STEPS - 1
        block = iterate_square(
            block, math.sqrt(columns) if last else 1.0, f32 if last else bf16, 1 if last else 2
        )
    return (new_momentum, block[0])


def body_general(columns, momentum, gradient):
    grad_full = gradient.astype(f32)
    new_momentum = momentum_decay * momentum + grad_full
    current = grad_full + momentum_decay * new_momentum
    for _ in range(STEPS):
        current = iterate_general(current)
    return (new_momentum, math.sqrt(columns) * current)


def solution(mesh):
    row_devices, column_devices = mesh.shape["dp"], mesh.shape["shard"]
    spec = P("dp", "shard")

    def sharded(body):
        return jax.shard_map(body, mesh=mesh, in_specs=(spec, spec), out_specs=(spec, spec), check_vma=False)

    def general(momentum, gradient):
        return sharded(functools.partial(body_general, momentum.shape[1]))(momentum, gradient)

    def square(momentum, gradient):
        return sharded(functools.partial(body_square, momentum.shape[1]))(momentum, gradient)

    if (row_devices, column_devices) != (ROW_DEVICES, COLUMN_DEVICES):
        return general
    return square
```

```python
import functools
import math

import jax
import jax.numpy as jnp
from jax import lax
from jax.experimental import pallas as pl
from jax.experimental.pallas import tpu as pltpu
from jax.sharding import PartitionSpec as P


STEPS = 2


momentum_decay = 0.95
linear_term = 3.4445
cubic_term = -4.775
quintic_term = 2.0315

f32, bf16 = jnp.float32, jnp.bfloat16


def dot_nn(a, b):
    return lax.dot_general(a, b, (((1,), (0,)), ((), ())), preferred_element_type=f32)


def dot_nt(a, b):
    return lax.dot_general(a, b, (((1,), (1,)), ((), ())), preferred_element_type=f32)


def iterate_general(current):
    matrix = current.astype(bf16)
    column_panel = lax.all_gather(matrix, "dp", axis=0, tiled=True)
    summed_part = lax.psum_scatter(dot_nt(matrix, column_panel), "shard", scatter_dimension=0, tiled=True)
    gram_part = summed_part.astype(bf16)
    gram_panel = lax.all_gather(gram_part, "shard", axis=0, tiled=True)
    square_sum = lax.psum(jnp.sum(jnp.square(gram_part.astype(f32))), ("dp", "shard"))
    inverse_norm = lax.rsqrt(square_sum)
    root_scale = jnp.sqrt(inverse_norm)
    matrix_full = matrix.astype(f32)
    first = dot_nn(gram_panel, column_panel)
    mixture = (
        cubic_term * root_scale * matrix_full + quintic_term * root_scale * inverse_norm * first
    ).astype(bf16)
    second = dot_nn(gram_panel, lax.all_gather(mixture, "dp", axis=0, tiled=True))
    return linear_term * root_scale * matrix_full + inverse_norm * second


def x_bit(i):
    return (i >> 1) & 1


def y_bit(i):
    return (i >> 2) & 1


def x_pick(i):
    return i ^ 2 ^ x_bit(i)


def y_pick(i):
    return i ^ 4 ^ (x_bit(i) ^ y_bit(i))


ROW_DEVICES = 8
COLUMN_DEVICES = 4
VMEM_LIMIT = 16 << 20
CORE = [(i, i ^ 1) for i in range(ROW_DEVICES)]
TAKE_X = [(x_pick(i), i) for i in range(ROW_DEVICES)]
TAKE_Y = [(y_pick(i), i) for i in range(ROW_DEVICES)]
GIVE_X = [(i, x_pick(i)) for i in range(ROW_DEVICES)]
GIVE_Y = [(i, y_pick(i)) for i in range(ROW_DEVICES)]


def over_dp(value, pairs):
    return lax.ppermute(value, "dp", pairs)


def call(kernel, outs, args, scalars=(), scratch=(), flops=0, streamed=False):
    moved = sum(a.size * a.dtype.itemsize for a in [*args, *outs])
    vmem = pl.BlockSpec(memory_space=pltpu.VMEM)
    return pl.pallas_call(
        kernel,
        out_shape=outs,
        in_specs=[pl.BlockSpec(memory_space=pltpu.SMEM)] * len(scalars) + [vmem] * len(args),
        out_specs=[pl.BlockSpec(memory_space=pl.ANY) if streamed else vmem] * len(outs),
        scratch_shapes=list(scratch),
        compiler_params=pltpu.CompilerParams(vmem_limit_bytes=VMEM_LIMIT),
        cost_estimate=pl.CostEstimate(flops=flops, bytes_accessed=moved, transcendentals=0),
    )(*scalars, *[pltpu.with_memory_space_constraint(a, pltpu.VMEM) for a in args])


def rows_at(z, k, rows):
    return pl.ds(pl.multiple_of((z ^ k) * rows, rows), rows)


def split_rows(total, z, outs):
    rows = outs[0].shape[1]
    for k, out in enumerate(outs):
        out[...] = total[:, rows_at(z, k, rows), :].astype(out.dtype)


def own_gram_kernel(z_ref, core_ref, top, bottom, core_top, core_bottom, *rest):
    outs, total = rest[:-1], rest[-1]
    for q, (left, right) in enumerate([(top, top), (bottom, bottom), (bottom, top)]):
        total[q] = dot_nt(left[...], right[...])
    for core, (first, second) in enumerate([(core_top, core_bottom), (core_bottom, core_top)]):

        @pl.when(core_ref[0] == core)
        def _():
            total[3] = dot_nt(top[...], first[...])
            total[4] = dot_nt(bottom[...], second[...])

    split_rows(total, z_ref[0], outs)


def stacked(top, bottom):
    return jnp.concatenate([top[...], bottom[...]], axis=0)


def early_gram_kernel(z_ref, top, bottom, x_bottom, y_top, *rest):
    outs, total = rest[:-1], rest[-1]
    half = top.shape[0]
    own = stacked(top, bottom)
    for q, right in ((0, x_bottom), (3, y_top)):
        value = dot_nt(own, right[...])
        total[q], total[q + 1] = value[:half], value[half:]
    total[2] = dot_nt(x_bottom[...], y_top[...])
    split_rows(total, z_ref[0], outs)


def late_gram_kernel(z_ref, top, bottom, x_top, x_bottom, y_top, y_bottom, *rest):
    outs, total = rest[:-1], rest[-1]
    half = top.shape[0]
    own = stacked(top, bottom)
    for q, right in ((0, x_top), (5, y_bottom)):
        value = dot_nt(own, right[...])
        total[q], total[q + 1] = value[:half], value[half:]
    total[2] = dot_nt(x_top[...], y_top[...])
    value = dot_nt(stacked(x_top, x_bottom), y_bottom[...])
    total[3], total[4] = value[:half], value[half:]
    split_rows(total, z_ref[0], outs)


def gram(kernel, shape, scalars, halves):
    count, rows, columns = shape
    shape = (count, rows // COLUMN_DEVICES, columns)
    return call(
        kernel,
        [jax.ShapeDtypeStruct(shape, kind) for kind in (f32, bf16, f32, bf16)],
        halves,
        scalars,
        [pltpu.VMEM((count, rows, columns), f32)],
        2 * count * rows * columns * halves[0].shape[1],
    )


def own_assemble_kernel(z_ref, *refs):
    parts, (diagonal, beside) = refs[:-2], refs[-2:]
    rows, half = parts[0].shape[1:]
    for k, part in enumerate(parts):
        at = rows_at(z_ref[0], k, rows)
        lower = pl.ds(pl.multiple_of(half + at.start, rows), rows)
        diagonal[at, :half] = part[0]
        diagonal[lower, half:] = part[1]
        diagonal[lower, :half] = part[2]
        beside[at, :] = part[3]
        beside[lower, :] = part[4]
    diagonal[:half, half:] = diagonal[half:, :half].T


def own_assemble(z, parts):
    half = parts[0].shape[2]
    outs = [jax.ShapeDtypeStruct((2 * half, columns), bf16) for columns in (2 * half, half)]
    return call(own_assemble_kernel, outs, parts, [z])


def beside_kernel(core_ref, own, other, out):
    half = own.shape[1]
    for core in range(2):

        @pl.when(core_ref[0] == core)
        def _():
            like, unlike = slice(core * half, (core + 1) * half), slice((1 - core) * half, (2 - core) * half)
            out[:half, like] = own[:half]
            out[half:, unlike] = own[half:]
            out[unlike, :half] = other[:half].T
            out[like, half:] = other[half:].T


def beside_of(core, own, other):
    rows = own.shape[0]
    return call(beside_kernel, [jax.ShapeDtypeStruct((rows, rows), bf16)], [own, other], [core])[0]


def near_assemble_kernel(z_ref, *refs):
    parts, near, wholes = refs[:COLUMN_DEVICES], refs[COLUMN_DEVICES], refs[COLUMN_DEVICES + 1 :]
    count, rows, half = parts[0].shape
    for k, part in enumerate(parts):
        at = rows_at(z_ref[0], k, rows)
        lower = pl.ds(pl.multiple_of(half + at.start, rows), rows)
        near[at, :half] = part[0]
        near[lower, :half] = part[1]
        near[at, half:] = part[count - 2]
        near[lower, half:] = part[count - 1]
        for w, whole in enumerate(wholes):
            whole[:, at, :] = part[2 * w : count - 2 + 2 * w]


def near_assemble(z, parts, with_wholes):
    count, _, half = parts[0].shape
    outs = [jax.ShapeDtypeStruct((2 * half, 2 * half), bf16)]
    if with_wholes:
        outs += [jax.ShapeDtypeStruct((count - 2, half, half), bf16)] * 2
    return call(near_assemble_kernel, outs, parts, [z])


def pack_kernel(*refs):
    parts, (x_pack, y_pack) = refs[:-2], refs[-2:]
    rows = parts[0].shape[1]
    for k, part in enumerate(parts):
        x_pack[:, k * rows : (k + 1) * rows] = part[:-2]
        y_pack[:, k * rows : (k + 1) * rows] = part[2:]


def pack(parts):
    count, rows, half = parts[0].shape
    return call(pack_kernel, [jax.ShapeDtypeStruct((count - 2, len(parts) * rows, half), bf16)] * 2, parts)


def mirror_assemble_kernel(z_ref, *refs):
    x_early, y_early, *late, side, linked, crossed, x_late, y_late = refs
    rows, half = late[0].shape[1:]
    for shifts, x_part, y_part in zip(((0,), (1, 2), (3,)), late[::2], late[1::2]):
        for k, shift in enumerate(shifts):
            at = rows_at(z_ref[0], shift, rows)
            x_late[:, at, :] = x_part[:, k * rows : (k + 1) * rows]
            y_late[:, at, :] = y_part[:, k * rows : (k + 1) * rows]
    columns = [slice(k * half, (k + 1) * half) for k in range(4)]
    top, bottom = columns[0], columns[1]
    for k in range(2):
        side[top, columns[k]] = x_late[k].T
        side[bottom, columns[k]] = x_early[k].T
        side[top, columns[2 + k]] = y_early[1 + k].T
        side[bottom, columns[2 + k]] = y_late[3 + k].T
    linked[top, top] = x_late[2]
    linked[bottom, top] = x_early[2]
    linked[top, bottom] = y_early[0].T
    linked[bottom, bottom] = y_late[2].T
    crossed[top, top] = x_late[3]
    crossed[bottom, top] = x_late[4]
    crossed[top, bottom] = y_late[0].T
    crossed[bottom, bottom] = y_late[1].T


def mirror_assemble(z, mirrored):
    count, _, half = mirrored[-1].shape
    outs = [jax.ShapeDtypeStruct((2 * half, width * half), bf16) for width in (4, 2, 2)]
    return call(mirror_assemble_kernel, outs, mirrored, [z], [pltpu.VMEM((count, half, half), bf16)] * 2)


def product_kernel(n_grams, n_halves, has_sum, finish, tile, stream, *refs):
    refs = list(refs)
    if stream:
        streamed, held, arrived = refs[-3:]
        refs = refs[:-3] + [held]

        def column_copy(t):
            at = pl.ds(pl.multiple_of(t * tile, tile), tile)
            return pltpu.make_async_copy(held.at[:, at], streamed.at[:, at], arrived.at[t])

    if finish:
        inverse_norm = lax.rsqrt(jnp.sum(refs.pop(0)[...], axis=(0, 1), keepdims=True))
        root_scale = jnp.sqrt(inverse_norm)
        scales = finish(root_scale, inverse_norm)
    grams, refs = refs[:n_grams], refs[n_grams:]
    halves, refs = refs[:n_halves], refs[n_halves:]
    summed = refs.pop(0) if has_sum else None
    own, outs = (refs[:2], refs[2:]) if finish else (None, refs)
    columns = halves[0].shape[1]

    def column_tile(t, carry):
        at = pl.ds(pl.multiple_of(t * tile, tile), tile)
        gram = jnp.concatenate([g[...] for g in grams], axis=1)
        value = dot_nn(gram, jnp.concatenate([h[:, at] for h in halves], axis=0))
        if has_sum:
            value = value + summed[:, at]
        if finish:
            block = jnp.concatenate([own[0][:, at], own[1][:, at]], axis=0)
            value = scales[0] * block.astype(f32) + scales[1] * value
        rows = value.shape[0] // len(outs)
        for k, out in enumerate(outs):
            out[:, at] = value[k * rows : (k + 1) * rows].astype(out.dtype)
        if stream:
            column_copy(t).start()
        return carry

    lax.fori_loop(0, columns // tile, column_tile, 0)
    if stream:

        def wait(t, carry):
            column_copy(t).wait()
            return carry

        lax.fori_loop(0, columns // tile, wait, 0)


def product(grams, halves, summed=None, finish=None, dtype=f32, parts=1, wide=False):
    half, columns = halves[0].shape
    tile = columns if wide or columns % 256 else 256
    args = ([finish[1]] if finish else []) + list(grams) + list(halves)
    args += [] if summed is None else [summed]
    args += list(finish[2]) if finish else []
    outs = [jax.ShapeDtypeStruct((2 * half // parts, columns), dtype)] * parts
    stream = bool(finish) and parts == 1
    return call(
        functools.partial(
            product_kernel, len(grams), len(halves), summed is not None, finish and finish[0], tile, stream
        ),
        outs,
        args,
        scratch=[pltpu.VMEM(outs[0].shape, dtype), pltpu.SemaphoreType.DMA((columns // tile,))] if stream else (),
        streamed=stream,
        flops=4 * half * half * columns * len(halves),
    )


def exchanged(value, distance):
    return lax.ppermute(value, "shard", [(z, z ^ distance) for z in range(COLUMN_DEVICES)])


def total_of(value):
    value = value + over_dp(value, CORE)
    x_side, y_side, diagonal = (over_dp(value, [(i, i ^ k) for i in range(ROW_DEVICES)]) for k in (2, 4, 6))
    return (value + x_side) + (y_side + diagonal)


def gather(block):
    top, bottom = block
    x_bottom, y_top = over_dp(bottom, TAKE_X), over_dp(top, TAKE_Y)
    x_top, y_bottom = over_dp(top, TAKE_X), over_dp(bottom, TAKE_Y)
    core = over_dp(top, CORE), over_dp(bottom, CORE)
    d_oth_bottom, d_sel_top = over_dp(x_bottom, GIVE_Y), over_dp(y_top, GIVE_X)
    x_oth_bottom, y_oth_top = over_dp(x_bottom, CORE), over_dp(y_top, CORE)
    x_oth_top, y_oth_bottom = over_dp(x_top, CORE), over_dp(y_bottom, CORE)
    side = x_oth_top, x_oth_bottom, y_oth_top, y_oth_bottom
    crossed = over_dp(d_oth_bottom, CORE), over_dp(d_sel_top, CORE)
    return core, (x_bottom, y_top), (x_top, y_bottom), side, (d_sel_top, d_oth_bottom), crossed


def add_kernel(kept, *refs):
    total = kept[...]
    for piece in refs[:-1]:
        total = total + piece[...].astype(f32)
    refs[-1][...] = total.astype(bf16)


def reduce_parts(pieces):
    kept, one, passed, three = pieces
    three, one = exchanged(three, 1), exchanged(one, 1)
    out = jax.ShapeDtypeStruct(kept.shape, bf16)
    (two,) = call(add_kernel, [out], [passed, three])
    two = exchanged(two, 2)
    return call(add_kernel, [out], [kept, one, two])[0]


def squares_kernel(weights, *refs):
    *parts, before, out = refs
    total = before[...]
    for part, part_weights in zip(parts, weights):
        for weight in sorted(set(part_weights)):
            square = sum(jnp.square(part[q].astype(f32)) for q, w in enumerate(part_weights) if w == weight)
            square = sum(square[:, k : k + 128] for k in range(0, square.shape[1], 128))
            total = total + weight * jnp.sum(square.reshape(-1, 8, 128), axis=0)
    out[...] = total


def squares_of(parts, weights, before):
    out = jax.ShapeDtypeStruct(before.shape, f32)
    return call(functools.partial(squares_kernel, weights), [out], [*parts, before])[0]


def spread(part):
    two, one = exchanged(part, 2), exchanged(part, 1)
    three = exchanged(two, 1)
    return [part, one, two, three]


def iterate_square(matrix, gain, dtype, parts):
    z = lax.axis_index("shard").reshape(1)
    side_index = (lax.axis_index("dp") & 1).reshape(1)
    core, one, two, side, linked, crossed = gather(matrix)
    (x_bottom, y_top), (x_top, y_bottom) = one, two
    half = matrix[0].shape[0]
    own_pieces = gram(own_gram_kernel, (5, half, half), [z, side_index], [*matrix, *core])
    own_part = reduce_parts(own_pieces)
    own_parts = spread(own_part)
    early_pieces = gram(early_gram_kernel, (5, half, half), [z], [*matrix, x_bottom, y_top])
    early_part = reduce_parts(early_pieces)
    late_pieces = gram(
        late_gram_kernel, (7, half, half), [z], [*matrix, x_top, x_bottom, y_top, y_bottom]
    )
    late_part = reduce_parts(late_pieces)
    early_parts = spread(early_part)
    late_parts = spread(late_part)
    zeros = jnp.zeros((8, 128), f32)
    last_squares = exchanged(squares_of([late_part], [(2.0,) * 7], zeros), 3)
    weights = [(1.0, 1.0, 2.0, 2.0, 2.0)] * 4 + [(2.0,) * 5] * 4 + [(2.0,) * 7] * 3
    squares = squares_of([*own_parts, *early_parts, *late_parts[:3]], weights, last_squares)
    squares = total_of(squares)
    near_one, x_whole, y_whole = near_assemble(z, early_parts, True)
    early = over_dp(x_whole, GIVE_X), over_dp(y_whole, GIVE_Y)
    late = []
    for shifts in ((0,), (1, 2), (3,)):
        x_part, y_part = late_parts[shifts[0]][:-2], late_parts[shifts[0]][2:]
        if len(shifts) > 1:
            x_part, y_part = pack([late_parts[k] for k in shifts])
        late += [over_dp(x_part, GIVE_X), over_dp(y_part, GIVE_Y)]
    own, beside = own_assemble(z, own_parts)
    beside = beside_of(side_index, beside, over_dp(beside, CORE))
    (near_two,) = near_assemble(z, late_parts, False)
    side_gram, linked_gram, crossed_gram = mirror_assemble(z, [*early, *late])

    def mixing(root_scale, inverse_norm):
        return cubic_term * root_scale, quintic_term * root_scale * inverse_norm

    def ending(root_scale, inverse_norm):
        return gain * linear_term * root_scale, gain * inverse_norm

    (first,) = product([own, beside], [*matrix, *core])
    (first,) = product([near_one, near_two], [*one, *two], first)
    mixture = product(
        [side_gram, linked_gram, crossed_gram],
        [*side, *linked, *crossed],
        first,
        (mixing, squares, matrix),
        bf16,
        2,
        True,
    )
    core, one, two, side, linked, crossed = gather(mixture)
    (second,) = product([own, beside], [*mixture, *core])
    (second,) = product([near_one], one, second)
    (second,) = product([near_two, side_gram], [*two, *side], second)
    (second,) = product([linked_gram], linked, second, wide=True)
    return product([crossed_gram], crossed, second, (ending, squares, matrix), dtype, parts, parts == 2)


def current_of(momentum, gradient):
    grad_full = gradient.astype(f32)
    new_momentum = momentum_decay * momentum + grad_full
    return new_momentum, grad_full + momentum_decay * new_momentum


def body_square(columns, momentum, gradient):
    half = momentum.shape[0] // 2
    block = [
        current_of(momentum[rows], gradient[rows])[1].astype(bf16)
        for rows in (slice(0, half), slice(half, None))
    ]
    new_momentum, _ = current_of(*lax.optimization_barrier((momentum, gradient)))
    for iteration in range(STEPS):
        last = iteration == STEPS - 1
        block = iterate_square(
            block, math.sqrt(columns) if last else 1.0, f32 if last else bf16, 1 if last else 2
        )
    return (new_momentum, block[0])


def body_general(columns, momentum, gradient):
    grad_full = gradient.astype(f32)
    new_momentum = momentum_decay * momentum + grad_full
    current = grad_full + momentum_decay * new_momentum
    for _ in range(STEPS):
        current = iterate_general(current)
    return (new_momentum, math.sqrt(columns) * current)


def solution(mesh):
    row_devices, column_devices = mesh.shape["dp"], mesh.shape["shard"]
    spec = P("dp", "shard")

    def sharded(body):
        return jax.shard_map(body, mesh=mesh, in_specs=(spec, spec), out_specs=(spec, spec), check_vma=False)

    def general(momentum, gradient):
        return sharded(functools.partial(body_general, momentum.shape[1]))(momentum, gradient)

    def square(momentum, gradient):
        return sharded(functools.partial(body_square, momentum.shape[1]))(momentum, gradient)

    if (row_devices, column_devices) != (ROW_DEVICES, COLUMN_DEVICES):
        return general
    return square
```
